32 devices in a mesh: region: 4 (over z), tracer: 2 (over x), sect: 4 (over y, core).
Axes of the slice: x: 2, y: 2, z: 4, core: 2. Of those that a mesh axis runs over, the one named last changes fastest.
Arguments:
- solute_concentration: float32 [16, 96, 32, 128], P('tracer', 'region', 'sect'), may hold values from 0.5 to 2
- thermal_anomaly: float32 [96, 32, 128], P('region', 'sect'), may hold values from -6 to 6
- eastward_flow_speed: float32 [96, 32, 128], P('region', 'sect'), may hold values from -1 to 1
- northward_flow_speed: float32 [96, 32, 128], P('region', 'sect'), may hold values from -1 to 1
- submerged_layers: int32 [96, 32], P('region', 'sect'), may hold values from 0 to 128, as said below
- interaction_matrix: float32 [16, 16], replicated, may hold values from -1.5 to 1.5
- bloom_yields: float32 [16], replicated, may hold values from -8 to 8
Outputs:
- tracers_next: float32 [16, 96, 32, 128], P('tracer', 'region', 'sect')
- temperature_next: float32 [96, 32, 128], P('region', 'sect')
The draws below stay inside these ranges and needn't reach their ends.
Inputs may be any that keep to these rules, and one draw needn't show every extreme that they name: `submerged_layers`: land (0) forms a few contiguous masses, with shallow shelves around them; columns far from land have all 128 levels.
All inputs are finite; a program needn't handle non-finite values.
Results may differ from the reference program's by a relative error of at most 0.0001.
Values sent between devices are 32-bit elements; how exact they have to be, the bound alone decides.
A program may use at most 64 MiB of HBM per device.

```python
import jax
import jax.numpy as jnp
from jax import lax

NTR = 16
DEPTH_LAYERS = 128
STEPS = 3
SUB = 4
GRID_EXTENT_EAST = 96
GRID_EXTENT_NORTH = 32


def draw_submerged_layers(key, part):
    keys = jax.random.split(jax.random.fold_in(key, 7), 4)
    count = 6
    centre_x = jax.random.randint(keys[0], (count,), 0, GRID_EXTENT_EAST)
    centre_y = jax.random.randint(keys[1], (count,), 0, GRID_EXTENT_NORTH)
    radius = jax.random.randint(keys[2], (count,), 3, 10)
    places_x = jnp.arange(GRID_EXTENT_EAST, dtype=jnp.int32)[:, None, None]
    places_y = jnp.arange(GRID_EXTENT_NORTH, dtype=jnp.int32)[None, :, None]
    dist_x = jnp.abs(places_x - centre_x[None, None, :])
    dist_x = jnp.minimum(dist_x, GRID_EXTENT_EAST - dist_x)
    dist_y = jnp.abs(places_y - centre_y[None, None, :])
    dist_y = jnp.minimum(dist_y, GRID_EXTENT_NORTH - dist_y)
    unit_x = dist_x * 64 // GRID_EXTENT_EAST
    unit_y = dist_y * 64 // GRID_EXTENT_NORTH
    excess = unit_x * unit_x + unit_y * unit_y - radius[None, None, :] * radius[None, None, :]
    nearest = jnp.min(excess, axis=2)
    jitter = jax.random.randint(keys[3], (GRID_EXTENT_EAST, GRID_EXTENT_NORTH), 0, DEPTH_LAYERS // 8 + 1)
    depth = jnp.minimum(DEPTH_LAYERS, DEPTH_LAYERS * jnp.maximum(nearest, 0) // 32 + 1 + jitter)
    return jnp.where(nearest < 0, 0, depth).astype(jnp.int32)


def block_levels(own_key, extent, cuts, smallest, largest):
    gain, own = 1.0, jax.random.fold_in(own_key, 6)
    for axis_at, parts in cuts:
        draws = jnp.exp(jax.random.uniform(jax.random.fold_in(own, axis_at), (parts,), jnp.float32, smallest / len(cuts), largest / len(cuts)))
        gain = gain * jnp.repeat(draws, extent[axis_at] // parts).reshape([-1 if axis == axis_at else 1 for axis in range(len(extent))])
    return gain


def noise(own_key, dims, scale, most, cuts=(), kind=jnp.bfloat16):
    gain = block_levels(own_key, dims, cuts, -0.22, 0.18) if cuts else 1.0
    drawn = jax.random.normal(own_key, dims, jnp.float32) * scale * gain
    return jnp.minimum(jnp.maximum(drawn, -most), most).astype(kind)


def setup_inputs(seed: int = 0) -> dict:
    arg_keys = jax.random.split(jax.random.key(seed), 8)
    return {
        "solute_concentration": jnp.clip(0.5 + 1.5 * jax.random.uniform(arg_keys[0], (NTR, GRID_EXTENT_EAST, GRID_EXTENT_NORTH, DEPTH_LAYERS), jnp.float32) ** block_levels(arg_keys[0], (NTR, GRID_EXTENT_EAST, GRID_EXTENT_NORTH, DEPTH_LAYERS), ((0, 2), (1, 4), (2, 4)), -0.2, 0.2), 0.5, 2.0),
        "thermal_anomaly": noise(arg_keys[1], (GRID_EXTENT_EAST, GRID_EXTENT_NORTH, DEPTH_LAYERS), 1.0, 6.0, ((0, 4), (1, 4)), jnp.float32),
        "eastward_flow_speed": jnp.clip(jax.random.uniform(arg_keys[2], (GRID_EXTENT_EAST, GRID_EXTENT_NORTH, DEPTH_LAYERS), jnp.float32, -1.0, 1.0) * block_levels(arg_keys[2], (GRID_EXTENT_EAST, GRID_EXTENT_NORTH, DEPTH_LAYERS), ((0, 4), (1, 4)), -0.4, 0.0), -1.0, 1.0),
        "northward_flow_speed": jnp.clip(jax.random.uniform(arg_keys[3], (GRID_EXTENT_EAST, GRID_EXTENT_NORTH, DEPTH_LAYERS), jnp.float32, -1.0, 1.0) * block_levels(arg_keys[3], (GRID_EXTENT_EAST, GRID_EXTENT_NORTH, DEPTH_LAYERS), ((0, 4), (1, 4)), -0.4, 0.0), -1.0, 1.0),
        "submerged_layers": draw_submerged_layers(jax.random.fold_in(arg_keys[7], 71), 0),
        "interaction_matrix": noise(arg_keys[5], (NTR, NTR), NTR ** -0.5, 1.5, (), jnp.float32),
        "bloom_yields": noise(arg_keys[6], (NTR,), 2.0, 8.0, (), jnp.float32),
    }


TIME_STEP = 0.2
REACT_STEP = 0.1
GROWTH_MAX = 1.0
HALF_SAT = 0.5
WATER_ATT = 3.0
CHL_ATT = 2.0
HEAT_GAIN = 0.5


def upwind_global(field, east_flux, north_flux):
    flux_x = jnp.maximum(east_flux, 0.0) * field + jnp.minimum(east_flux, 0.0) * jnp.roll(field, -1, axis=-3)
    flux_y = jnp.maximum(north_flux, 0.0) * field + jnp.minimum(north_flux, 0.0) * jnp.roll(field, -1, axis=-2)
    return flux_x - jnp.roll(flux_x, 1, axis=-3) + flux_y - jnp.roll(flux_y, 1, axis=-2)


def light(chl_abs, upper_ones):
    layer_total = chl_abs.shape[-1]
    cells = chl_abs.reshape(-1, layer_total)
    above = jnp.dot(cells, upper_ones, precision=lax.Precision.HIGHEST, preferred_element_type=jnp.float32)
    above = above.reshape(chl_abs.shape)
    depth = jnp.arange(layer_total, dtype=jnp.float32) + 0.5
    return jnp.exp(-(WATER_ATT / layer_total * depth + CHL_ATT / layer_total * (above + 0.5 * chl_abs)))


def react(mixture, interaction_matrix, bloom_yields, upper_ones):
    for substep in range(SUB):
        chl_abs = jnp.abs(mixture[1])
        nutrient = mixture[0]
        rate = GROWTH_MAX * light(chl_abs, upper_ones) * nutrient / (jnp.abs(nutrient) + HALF_SAT)
        linear = jnp.einsum("ab,bxyk->axyk", interaction_matrix, mixture, precision=lax.Precision.HIGHEST)
        tendency = linear + bloom_yields[:, None, None, None] * (rate * mixture[2])[None]
        mixture = mixture + REACT_STEP * tendency
    chl_abs = jnp.abs(mixture[1])
    heating = HEAT_GAIN * chl_abs * light(chl_abs, upper_ones)
    return mixture, heating


def reference(solute_concentration, thermal_anomaly, eastward_flow_speed, northward_flow_speed, submerged_layers, interaction_matrix, bloom_yields):
    water_mask = (jnp.arange(DEPTH_LAYERS, dtype=jnp.int32)[None, None, :] < submerged_layers[:, :, None]).astype(jnp.float32)
    east_flux = eastward_flow_speed * water_mask * jnp.roll(water_mask, -1, axis=0)
    north_flux = northward_flow_speed * water_mask * jnp.roll(water_mask, -1, axis=1)
    upper_ones = (jnp.arange(DEPTH_LAYERS)[:, None] < jnp.arange(DEPTH_LAYERS)[None, :]).astype(jnp.float32)
    mixture = solute_concentration
    warming_tendency = thermal_anomaly
    for section_index in range(STEPS):
        mixture = water_mask * (mixture - TIME_STEP * upwind_global(mixture, east_flux, north_flux))
        warming_tendency = water_mask * (warming_tendency - TIME_STEP * upwind_global(warming_tendency, east_flux, north_flux))
        mixture, heating = react(mixture, interaction_matrix, bloom_yields, upper_ones)
        warming_tendency = warming_tendency + TIME_STEP * water_mask * heating
    return mixture, warming_tendency
```

```python
import functools

import jax
import jax.numpy as jnp
from jax import lax
from jax.experimental import pallas as pl
from jax.experimental.pallas import tpu as pltpu
from jax.sharding import PartitionSpec as P

STEPS = 3
SUB = 4

TIME_STEP = 0.2
REACT_STEP = 0.1
GROWTH_MAX = 1.0
HALF_SAT = 0.5
WATER_ATT = 3.0
CHL_ATT = 2.0
HEAT_GAIN = 0.5

MESH = pl.DeviceIdType.MESH
HIGHEST = lax.Precision.HIGHEST
EAST, WEST, NORTH, SOUTH = range(4)


def iota(shape, dim):
    return lax.broadcasted_iota(jnp.int32, shape, dim)


def exact_dot(a, b, dims=((1,), (0,))):
    return lax.dot_general(
        a, b, (dims, ((), ())), precision=HIGHEST, preferred_element_type=jnp.float32
    )


def halves(x):
    high = x.astype(jnp.bfloat16)
    return high, (x - high.astype(jnp.float32)).astype(jnp.bfloat16)


def half_dot(a, b):
    return jnp.dot(a, b, preferred_element_type=jnp.float32)


def dot3(a, b):
    return half_dot(a[0], b[0]) + half_dot(a[1], b[0]) + half_dot(a[0], b[1])


def tables(rates_ref, yields_ref, tracers, wide, Y):
    rows = tracers * Y
    spread = (iota((rows, tracers), 0) // Y == iota((rows, tracers), 1)).astype(jnp.float32)
    same = iota((rows, rows), 0) % Y == iota((rows, rows), 1) % Y
    full = exact_dot(exact_dot(spread, rates_ref[...]), spread, ((1,), (1,)))
    full = jnp.where(same, full, 0.0) * REACT_STEP
    diagonal = (iota((rows, rows), 0) == iota((rows, rows), 1)).astype(jnp.float32)
    one = diagonal + full
    two = exact_dot(one, one)
    three = exact_dot(two, one)
    four = exact_dot(two, two)
    source = [
        exact_dot(spread * yields_ref[...], jnp.ones((tracers, wide), jnp.float32)) * REACT_STEP
    ]
    for power in (one, two, three):
        source.append(exact_dot(power, source[0]))
    head = jnp.concatenate([power[: 3 * Y] for power in (one, two, three)], axis=0)
    shape = (rows, wide)
    lane = iota(shape, 1)
    inject = jnp.zeros(shape, jnp.float32)
    for sub in range(SUB):
        hit = jnp.logical_and(lane // Y == sub, lane % Y == iota(shape, 0) % Y)
        inject = inject + jnp.where(hit, source[SUB - 1 - sub], 0.0)
    return head, four, inject[:, : SUB * Y], [v[: 3 * Y] for v in source[: SUB - 1]]


def stack(flat, wide):
    return jnp.concatenate(
        [flat[:, i * wide : (i + 1) * wide] for i in range(flat.shape[1] // wide)], axis=0
    )


def unstack(tall, Y):
    return jnp.concatenate(
        [tall[i * Y : (i + 1) * Y] for i in range(tall.shape[0] // Y)], axis=1
    )


def plan(span):
    return (3, (0, 2, 1)) if span % 3 == 0 else (1, (0,))


def kernel(
    regions, groups, sects,
    solute, heat_hbm, east_hbm, north_hbm, layers_hbm, rates_hbm, yields_hbm,
    tracers_out, heat_out,
    layers_in, rates_ref, yields_ref,
    state, ysend, yrecv, coef, final,
    in_send, in_recv, halo_send, halo_recv, out_send, out_recv, local_sem, load_sem,
):
    region, group, sect = (lax.axis_index(a) for a in ("region", "tracer", "sect"))
    own, wide, Y = solute.shape[0], solute.shape[2], layers_in.shape[0]
    tracers = own * groups
    block = heat_hbm.shape[0] // groups
    span = block // Y
    fields = tracers + 1
    every = fields + 3

    def place(reg, t):
        return t + (reg % 2) * (groups - 1 - 2 * t)

    part = place(region, group)
    last = groups - 1
    next_region = lax.rem(region + 1, regions)
    past_region = lax.rem(region + regions - 1, regions)
    east_region = jnp.where(part == last, next_region, region)
    west_region = jnp.where(part == 0, past_region, region)
    east_part = jnp.where(part == last, 0, part + 1)
    west_part = jnp.where(part == 0, last, part - 1)
    beside = {
        EAST: {"region": east_region, "tracer": place(east_region, east_part)},
        WEST: {"region": west_region, "tracer": place(west_region, west_part)},
        NORTH: {"sect": lax.rem(sect + 1, sects)},
        SOUTH: {"sect": lax.rem(sect + sects - 1, sects)},
    }
    peers = [lax.rem(group + d, groups) for d in range(1, groups)]

    def rows_of(t):
        return pl.ds(pl.multiple_of(place(region, t) * block, Y), block)

    mine = rows_of(group)
    slot = pl.ds(group * own, own)
    inner = pl.ds(Y, block)

    barrier = pltpu.get_barrier_semaphore()
    for peer in peers:
        pl.semaphore_signal(barrier, inc=1, device_id={"tracer": peer}, device_id_type=MESH)
    for side in range(4):
        pl.semaphore_signal(barrier, inc=1, device_id=beside[side], device_id_type=MESH)
    keep = pltpu.make_async_copy(
        solute.at[:, mine, :], state.at[0, slot, inner, :], local_sem.at[0, 0]
    )
    keep.start()
    loads = []
    for i, (source_ref, target_ref) in enumerate(
        (
            (layers_hbm, layers_in),
            (rates_hbm, rates_ref),
            (yields_hbm, yields_ref),
            (heat_hbm.at[mine, :], state.at[0, tracers, inner, :]),
            (east_hbm.at[mine, :], state.at[0, fields, inner, :]),
            (north_hbm.at[mine, :], state.at[0, fields + 1, inner, :]),
        )
    ):
        copy = pltpu.make_async_copy(source_ref, target_ref, load_sem.at[i])
        copy.start()
        loads.append(copy)
    pl.semaphore_wait(barrier, groups - 1 + 4)

    chunks, order = plan(span)
    deep = span // chunks
    piece = deep * Y

    def part_of(t, c):
        return pl.ds(pl.multiple_of(place(region, t) * block + c * piece, Y), piece)

    arriving = {}
    for i, c in enumerate(order):
        for d, peer in enumerate(peers):
            copy = pltpu.make_async_remote_copy(
                src_ref=solute.at[:, part_of(peer, c), :],
                dst_ref=state.at[0, slot, pl.ds(Y + c * piece, piece), :],
                send_sem=in_send.at[d, c],
                recv_sem=in_recv.at[d, c],
                device_id={"tracer": peer},
                device_id_type=MESH,
            )
            copy.start()
            arriving[c, d] = copy

    for copy in loads:
        copy.wait()
    total = layers_in.shape[1] * Y
    pick = (iota((total, layers_in.shape[1]), 0) // Y == iota((total, layers_in.shape[1]), 1))
    depth = lax.dot_general(
        pick.astype(jnp.bfloat16),
        layers_in[...].astype(jnp.float32).astype(jnp.bfloat16),
        (((1,), (1,)), ((), ())),
        preferred_element_type=jnp.float32,
    )
    depth = jnp.where(iota((total, Y), 0) % Y == iota((total, Y), 1), depth, 0.0)
    depth = half_dot(depth.astype(jnp.bfloat16), jnp.ones((Y, wide), jnp.bfloat16))
    coef[5] = (iota((total, wide), 1).astype(jnp.float32) < depth).astype(jnp.float32)
    state[0, fields + 2, inner, :] = coef[5, mine, :]

    head, four, inject, source = tables(rates_ref, yields_ref, tracers, wide, Y)
    head, four, inject = halves(head), halves(four), halves(inject)
    upper = (iota((wide, wide), 0) < iota((wide, wide), 1)).astype(jnp.bfloat16)
    level = iota((piece, wide), 1).astype(jnp.float32) + 0.5
    tile = (1, deep)
    source = [jnp.tile(v, tile) for v in source]

    def light(chl_abs):
        high, low = halves(chl_abs)
        above = half_dot(high, upper) + half_dot(low, upper)
        return jnp.exp(
            -(WATER_ATT / wide * level + CHL_ATT / wide * (above + 0.5 * chl_abs))
        )

    sent = []

    def exchange(step, c):
        count = every if step == 0 else fields
        some = pl.ds(0, count)
        moves = {}
        if c == chunks - 1:
            moves[EAST] = (
                state.at[step, some, pl.ds(block, Y), :],
                state.at[step, some, pl.ds(0, Y), :],
            )
        if c == 0:
            moves[WEST] = (
                state.at[step, some, pl.ds(Y, Y), :],
                state.at[step, some, pl.ds(block + Y, Y), :],
            )

        def send(moves):
            for side, (source_ref, target_ref) in moves.items():
                copy = pltpu.make_async_remote_copy(
                    src_ref=source_ref,
                    dst_ref=target_ref,
                    send_sem=halo_send.at[step, c, side],
                    recv_sem=halo_recv.at[step, c, side],
                    device_id=beside[side],
                    device_id_type=MESH,
                )
                copy.start()
                sent.append(copy)
                halos[step, c, side] = copy

        send(moves)
        for f in range(count):
            for side, y in ((0, 0), (1, Y - 1)):
                ysend[step, c, side, f] = state[
                    step, f, pl.ds(Y + c * piece + y, deep, stride=Y), :
                ]
        moves = {
            NORTH: (ysend.at[step, c, 1, some], yrecv.at[step, c, 1, some]),
            SOUTH: (ysend.at[step, c, 0, some], yrecv.at[step, c, 0, some]),
        }
        send(moves)

    halos = {}

    def beside_y(step, value, x, first, count):
        at = (count, Y, wide)
        row = iota(at, 1)
        some = pl.ds(first, count)
        above = jnp.broadcast_to(yrecv[step, x // deep, 0, some, pl.ds(x % deep, 1), :], at)
        below = jnp.broadcast_to(yrecv[step, x // deep, 1, some, pl.ds(x % deep, 1), :], at)
        up = jnp.where(row == Y - 1, above, pltpu.roll(value, Y - 1, 1))
        down = jnp.where(row == 0, below, pltpu.roll(value, 1, 1))
        return up, down

    keep.wait()
    for c in order:
        for d in range(len(peers)):
            arriving[c, d].wait_recv()
        exchange(0, c)

    leaving = []

    def leave(c):
        rows = pl.ds(c * piece, piece)
        out_rows = part_of(group, c)
        for d, peer in enumerate(peers):
            pairs = (
                (final.at[pl.ds(peer * own, own), rows, :], tracers_out.at[:, out_rows, :]),
                (final.at[tracers, rows, :], heat_out.at[out_rows, :]),
            )
            for i, (source_ref, target_ref) in enumerate(pairs):
                copy = pltpu.make_async_remote_copy(
                    src_ref=source_ref,
                    dst_ref=target_ref,
                    send_sem=out_send.at[d, c, i],
                    recv_sem=out_recv.at[d, c, i],
                    device_id={"tracer": peer},
                    device_id_type=MESH,
                )
                copy.start()
                leaving.append(copy)
        pairs = (
            (final.at[slot, rows, :], tracers_out.at[:, out_rows, :]),
            (final.at[tracers, rows, :], heat_out.at[out_rows, :]),
        )
        for i, (source_ref, target_ref) in enumerate(pairs):
            copy = pltpu.make_async_copy(source_ref, target_ref, local_sem.at[c, 1 + i])
            copy.start()
            leaving.append(copy)

    def advance(step, c):
        columns, heats, wets = [], [], []
        for x in range(c * deep, (c + 1) * deep):
            here = pl.ds((x + 1) * Y, Y)
            ahead = pl.ds((x + 2) * Y, Y)
            behind = pl.ds(x * Y, Y)
            cell = pl.ds(x * Y, Y)
            if step == 0:
                speed_wet = state[0, pl.ds(fields + 1, 2), here, :]
                up, down = beside_y(0, speed_wet, x, fields + 1, 2)
                wet = speed_wet[1]
                east = state[0, fields, here, :] * wet * state[0, fields + 2, ahead, :]
                west = state[0, fields, behind, :] * state[0, fields + 2, behind, :] * wet
                north = speed_wet[0] * wet * up[1]
                south = down[0] * down[1] * wet
                scaled = TIME_STEP * wet
                coef[0, cell, :] = wet - scaled * (
                    jnp.maximum(east, 0.0) - jnp.minimum(west, 0.0)
                    + jnp.maximum(north, 0.0) - jnp.minimum(south, 0.0)
                )
                coef[1, cell, :] = -scaled * jnp.minimum(east, 0.0)
                coef[2, cell, :] = scaled * jnp.maximum(west, 0.0)
                coef[3, cell, :] = -scaled * jnp.minimum(north, 0.0)
                coef[4, cell, :] = scaled * jnp.maximum(south, 0.0)
            value = state[step, pl.ds(0, fields), here, :]
            up, down = beside_y(step, value, x, 0, fields)
            moved = (
                coef[0, cell, :] * value
                + coef[1, cell, :] * state[step, pl.ds(0, fields), ahead, :]
                + coef[2, cell, :] * state[step, pl.ds(0, fields), behind, :]
                + coef[3, cell, :] * up
                + coef[4, cell, :] * down
            )
            columns.append(moved[:tracers].reshape(tracers * Y, wide))
            heats.append(moved[tracers])
            wets.append(state[0, fields + 2, here, :])
        mixed = jnp.concatenate(columns, axis=1)
        parts = halves(mixed)
        ahead_rows = dot3(head, parts)
        result = dot3(four, parts)
        rates = []
        for sub in range(SUB):
            if sub == 0:
                rows = mixed[: 3 * Y]
            else:
                rows = ahead_rows[(sub - 1) * 3 * Y : sub * 3 * Y]
                for i, rate in enumerate(rates):
                    rows = rows + source[sub - 1 - i] * jnp.concatenate([rate] * 3, axis=0)
            nutrient, chl, phyto = rows[:Y], rows[Y : 2 * Y], rows[2 * Y :]
            shade = unstack(light(jnp.abs(stack(chl, wide))), Y)
            rates.append(
                GROWTH_MAX * shade * nutrient / (jnp.abs(nutrient) + HALF_SAT) * phyto
            )
        result = result + dot3(inject, halves(jnp.concatenate(rates, axis=0)))
        chl_abs = jnp.abs(stack(result[Y : 2 * Y], wide))
        heating = HEAT_GAIN * chl_abs * light(chl_abs)
        heat = jnp.concatenate(heats, axis=0) + TIME_STEP * jnp.concatenate(wets, axis=0) * heating
        if step < STEPS - 1:
            target, base = state.at[step + 1], Y + c * piece
        else:
            target, base = final, c * piece
        for x in range(deep):
            target[pl.ds(0, tracers), pl.ds(base + x * Y, Y), :] = result[
                :, x * wide : (x + 1) * wide
            ].reshape(tracers, Y, wide)
        target[tracers, pl.ds(base, piece), :] = heat

    for step in range(STEPS):
        for c in order:
            for side in (NORTH, SOUTH):
                halos[step, c, side].wait_recv()
            if c == 0:
                halos[step, chunks - 1, EAST].wait_recv()
            if c == chunks - 1:
                halos[step, 0, WEST].wait_recv()
            advance(step, c)
            if step < STEPS - 1:
                exchange(step + 1, c)
            else:
                leave(c)
    for copy in leaving:
        copy.wait()
    for copy in sent + list(arriving.values()):
        copy.wait_send()

SHARE = 0
FIRST = 3


def wide_halves(x):
    high, low = halves(x)
    return jnp.concatenate([high, high, low], axis=1)


def tall_halves(x):
    high, low = halves(x)
    return jnp.concatenate([high, low, high], axis=0)


def pair_tables(rates_ref, yields_ref, tracers, wide, Y):
    rows = tracers * Y
    spread = (iota((rows, tracers), 0) // Y == iota((rows, tracers), 1)).astype(jnp.float32)
    same = iota((rows, rows), 0) % Y == iota((rows, rows), 1) % Y
    full = exact_dot(exact_dot(spread, rates_ref[...]), spread, ((1,), (1,)))
    full = jnp.where(same, full, 0.0) * REACT_STEP
    diagonal = (iota((rows, rows), 0) == iota((rows, rows), 1)).astype(jnp.float32)
    one = diagonal + full
    two = exact_dot(one, one)
    three = exact_dot(two, one)
    four = exact_dot(two, two)
    source = [
        exact_dot(spread * yields_ref[...], jnp.ones((tracers, wide), jnp.float32)) * REACT_STEP
    ]
    for power in (one, two, three):
        source.append(exact_dot(power, source[0]))
    powers = jnp.concatenate([power[: 3 * Y] for power in (one, two, three)] + [four], axis=0)
    shape = (rows, wide)
    lane = iota(shape, 1)
    inject = jnp.zeros(shape, jnp.float32)
    for sub in range(SUB):
        hit = jnp.logical_and(lane // Y == sub, lane % Y == iota(shape, 0) % Y)
        inject = inject + jnp.where(hit, source[SUB - 1 - sub], 0.0)
    return (
        wide_halves(powers),
        wide_halves(inject[:, : SUB * Y]),
        [v[: 3 * Y] for v in source],
    )


def pair_plan(half):
    low = -SHARE - STEPS
    ranges, at = [(half - STEPS, STEPS)], SHARE - STEPS
    while at < half - STEPS:
        size = min(STEPS, half - STEPS - at)
        ranges.append((at, size))
        at += size
    if SHARE:
        ranges.append((low, SHARE * 2))
    return low, ranges


def pair_kernel(
    regions, sects,
    solute, heat_hbm, east_hbm, north_hbm, layers_hbm, rates_hbm, yields_hbm,
    tracers_out, heat_out,
    layers_in, rates_ref, yields_ref, state, coef, wets, final,
    send_sem, recv_sem, local_sem,
):
    groups = 2
    region, group, sect = (lax.axis_index(a) for a in ("region", "tracer", "sect"))
    own, X, Y, wide = solute.shape
    half = X // groups
    tracers = own * groups
    fields = tracers + 1
    base = STEPS + 1
    low, ranges = pair_plan(half)
    reach = half - low
    odd = region % 2
    part = group + odd * (1 - 2 * group)
    peer = 1 - group

    def pick(flag, a, b):
        return a + flag * (b - a)

    def P(u, k, flag=part):
        return pick(flag, half + STEPS - u - k, u - low)

    def B(u, k, flag=part):
        return pick(flag, half - u - k, half + u)

    outer_region = lax.rem(region + pick(part, regions - 1, 1), regions)
    outer_part = 1 - part
    outer_odd = outer_region % 2
    beside = {"region": outer_region, "tracer": outer_part + outer_odd * (1 - 2 * outer_part)}
    north = {"sect": lax.rem(sect + 1, sects)}
    south = {"sect": lax.rem(sect + sects - 1, sects)}
    across = {"tracer": peer}
    mine, other = pl.ds(group * own, own), pl.ds(peer * own, own)

    barrier = pltpu.get_barrier_semaphore()
    for device in (across, beside, north, south):
        pl.semaphore_signal(barrier, inc=1, device_id=device, device_id_type=MESH)

    count = [0, 0]
    sent, leaving, arrivals = [], [], []

    def local(source_ref, target_ref):
        copy = pltpu.make_async_copy(source_ref, target_ref, local_sem.at[count[0]])
        count[0] += 1
        copy.start()
        return copy

    def remote(source_ref, target_ref, device):
        copy = pltpu.make_async_remote_copy(
            src_ref=source_ref,
            dst_ref=target_ref,
            send_sem=send_sem.at[count[1]],
            recv_sem=recv_sem.at[count[1]],
            device_id=device,
            device_id_type=MESH,
        )
        count[1] += 1
        copy.start()
        sent.append(copy)
        return copy

    raw = state.at[0]
    body = pl.ds(base, Y)
    tables_in = [
        local(layers_hbm, layers_in),
        local(rates_hbm, rates_ref),
        local(yields_hbm, yields_ref),
    ]
    p_all, b_all = P(low, reach), B(low, reach)
    in_block = pl.ds(b_all, reach)
    in_state = pl.ds(p_all, reach)
    extra = ((heat_hbm, tracers), (east_hbm, fields), (north_hbm, fields + 1))
    loads = [local(solute.at[:, in_block], raw.at[mine, in_state, body])]
    for ref, field in extra:
        loads.append(local(ref.at[in_block], raw.at[field, in_state, body]))

    with jax.named_scope('barrier'):
        pl.semaphore_wait(barrier, 4)

    def cross(u, k):
        return remote(
            solute.at[:, pl.ds(B(u, k, 1 - part), k)],
            raw.at[mine, pl.ds(P(u, k, 1 - part), k), body],
            across,
        )

    edge = half - STEPS
    edge_block = pl.ds(B(edge, STEPS), STEPS)
    edge_state = pl.ds(P(edge, STEPS), STEPS)
    past = pl.ds(pick(part, reach, 0), STEPS)
    crossing = [cross(*ranges[0])]
    outer = [remote(solute.at[:, edge_block], raw.at[mine, past, body], beside)]
    for ref, field in extra:
        outer.append(remote(ref.at[edge_block], raw.at[field, past, body], beside))
    crossing += [cross(*r) for r in ranges[1:]]
    sides = (
        (pl.ds(Y - STEPS, STEPS), pl.ds(base - STEPS, STEPS), north),
        (pl.ds(0, STEPS), pl.ds(base + Y, STEPS), south),
    )
    rows = []
    for block_rows, halo_rows, device in sides:
        rows.append(
            remote(
                solute.at[:, in_block, block_rows], raw.at[mine, in_state, halo_rows], device
            )
        )
        for ref, field in extra:
            rows.append(
                remote(ref.at[in_block, block_rows], raw.at[field, in_state, halo_rows], device)
            )

    def beside_rows(some, place):
        return [
            remote(
                raw.at[some, place, pl.ds(base + y, STEPS)],
                raw.at[some, place, halo_rows],
                device,
            )
            for y, (_, halo_rows, device) in zip((Y - STEPS, 0), sides)
        ]

    for copy in tables_in:
        copy.wait()
    total = X * Y
    pick_rows = iota((total, X), 0) // Y == iota((total, X), 1)
    depth = lax.dot_general(
        pick_rows.astype(jnp.bfloat16),
        layers_in[...].astype(jnp.float32).astype(jnp.bfloat16),
        (((1,), (1,)), ((), ())),
        preferred_element_type=jnp.float32,
    )
    depth = jnp.where(iota((total, Y), 0) % Y == iota((total, Y), 1), depth, 0.0)
    depth = half_dot(depth.astype(jnp.bfloat16), jnp.ones((Y, wide), jnp.bfloat16))
    wets[...] = (iota((total, wide), 1).astype(jnp.float32) < depth).astype(jnp.float32).reshape(
        X, Y, wide
    )
    wet_field = fields + 2
    raw[wet_field, in_state, body, :] = wets[in_block]
    outer.append(remote(raw.at[wet_field, edge_state, body], raw.at[wet_field, past, body], beside))
    rows += beside_rows(wet_field, in_state)

    with jax.named_scope('tables'):
        powers, inject, source = pair_tables(rates_ref, yields_ref, tracers, wide, Y)
    shape = (wide, wide)
    upper = (iota(shape, 0) < iota(shape, 1)).astype(jnp.float32)
    upper = upper + 0.5 * (iota(shape, 0) == iota(shape, 1)).astype(jnp.float32)
    upper = jnp.concatenate([upper.astype(jnp.bfloat16)] * 2, axis=0)
    level = (iota((Y, wide), 1).astype(jnp.float32) + 0.5) * (-WATER_ATT / wide)
    for copy in loads:
        copy.wait()

    def light(chl_abs):
        high, low_part = halves(chl_abs)
        above = half_dot(jnp.concatenate([high, low_part], axis=1), upper)
        tall = jnp.concatenate([level] * (chl_abs.shape[0] // Y), axis=0)
        return jnp.exp(tall - CHL_ATT / wide * above)

    done = set()
    passed = {}
    outer_rows = []

    def arrive(i):
        if ("x", i) in done:
            return
        done.add(("x", i))
        with jax.named_scope(f"x{i}"):
            crossing[i].wait_recv()
        u, k = ranges[i]
        some = pl.ds(P(u, k), k)
        if i == 0:
            outer.append(remote(raw.at[other, some, body], raw.at[other, past, body], beside))
        passed[i] = beside_rows(other, some)

    def arrive_outer():
        if "outer" in done:
            return
        done.add("outer")
        for i, copy in enumerate(outer):
            with jax.named_scope(f"outer{i}"):
                copy.wait_recv()
        outer_rows.extend(beside_rows(slice(None), pl.ds(P(half, STEPS), STEPS)))

    def ready(first, last):
        if "rows" not in done:
            done.add("rows")
            for i, copy in enumerate(rows):
                with jax.named_scope(f"rows{i}"):
                    copy.wait_recv()
        for i, (u, k) in enumerate(ranges):
            if u <= last and first < u + k:
                arrive(i)
                if ("y", i) not in done:
                    done.add(("y", i))
                    with jax.named_scope(f"passed{i}"):
                        for copy in passed[i]:
                            copy.wait_recv()
        if last >= half:
            arrive_outer()
            if "corner" not in done:
                done.add("corner")
                with jax.named_scope("corner"):
                    for copy in outer_rows:
                        copy.wait_recv()

    windows = [
        (base - STEPS + 1, base + Y + STEPS - 1 - Y),
        (base - 1, base + 1),
        (base,),
    ]

    def stencil(step, p, r):
        here = pl.ds(r, Y)
        up_rows, down_rows = pl.ds(r + 1, Y), pl.ds(r - 1, Y)
        if step == 0:
            wet = raw[wet_field, p, here, :]
            south_wet = raw[wet_field, p, down_rows, :]
            east = raw[fields, p, here, :] * wet * raw[wet_field, p + 1, here, :]
            west = raw[fields, p - 1, here, :] * raw[wet_field, p - 1, here, :] * wet
            up = raw[fields + 1, p, here, :] * wet * raw[wet_field, p, up_rows, :]
            down = raw[fields + 1, p, down_rows, :] * south_wet * wet
            scaled = TIME_STEP * wet
            c = [
                wet
                - scaled
                * (
                    jnp.maximum(east, 0.0) - jnp.minimum(west, 0.0)
                    + jnp.maximum(up, 0.0) - jnp.minimum(down, 0.0)
                ),
                -scaled * jnp.minimum(east, 0.0),
                scaled * jnp.maximum(west, 0.0),
                -scaled * jnp.minimum(up, 0.0),
                scaled * jnp.maximum(down, 0.0),
                scaled,
            ]
            for i, v in enumerate(c):
                coef[i, p, here, :] = v
        else:
            c = [coef[i, p, here, :] for i in range(6)]
        some = pl.ds(0, fields)
        moved = (
            c[0] * state[step, some, p, here, :]
            + c[1] * state[step, some, p + 1, here, :]
            + c[2] * state[step, some, p - 1, here, :]
            + c[3] * state[step, some, p, up_rows, :]
            + c[4] * state[step, some, p, down_rows, :]
        )
        return moved, c[5]

    def advance(*work):
        for step, u, k in work:
            if step == 0:
                ready(u - 1, u + k)
        with jax.named_scope("go" + "_".join(f"{s}:{u}:{k}" for s, u, k in work)):
            compute(work)

    def compute(work):
        tiles = []
        for step, u, k in work:
            p = P(u, k)
            for i in range(k):
                for r in windows[step]:
                    tiles.append((step, p + i, r))
        columns, heats, scales = [], [], []
        for step, p, r in tiles:
            moved, scaled = stencil(step, p, r)
            columns.append(moved[:tracers].reshape(tracers * Y, wide))
            heats.append(moved[tracers])
            scales.append(scaled)
        n = len(tiles)
        mixed = jnp.concatenate(columns, axis=1)
        ahead = half_dot(powers, tall_halves(mixed))
        block = 3 * Y
        result = ahead[3 * block :]

        def part_of(rows, i):
            return stack(rows[i * Y : (i + 1) * Y], wide)

        def spread(v, i):
            return jnp.concatenate([v[i * Y : (i + 1) * Y]] * n, axis=0)

        rates = []
        for sub in range(SUB):
            rows = mixed[:block] if sub == 0 else ahead[(sub - 1) * block : sub * block]
            value = []
            for i in range(3):
                v = part_of(rows, i)
                for j, rate in enumerate(rates):
                    v = v + spread(source[sub - 1 - j], i) * rate
                value.append(v)
            nutrient, chl, phyto = value
            rates.append(
                light(jnp.abs(chl)) * (nutrient / (jnp.abs(nutrient) + HALF_SAT) * phyto)
            )
        chl = part_of(result, 1)
        for j, rate in enumerate(rates):
            chl = chl + spread(source[SUB - 1 - j], 1) * rate
        chl_abs = jnp.abs(chl)
        flat = jnp.concatenate([unstack(rate, Y) for rate in rates], axis=0)
        result = result + half_dot(inject, tall_halves(flat))
        heat = jnp.concatenate(heats, axis=0) + HEAT_GAIN * (
            jnp.concatenate(scales, axis=0) * chl_abs * light(chl_abs)
        )
        for i, (step, p, r) in enumerate(tiles):
            value = result[:, i * wide : (i + 1) * wide].reshape(tracers, Y, wide)
            if step < STEPS - 1:
                here = pl.ds(r, Y)
                state[step + 1, pl.ds(0, tracers), p, here, :] = value
                state[step + 1, tracers, p, here, :] = heat[i * Y : (i + 1) * Y]
            else:
                final[pl.ds(0, tracers), p, :, :] = value
                final[tracers, p, :, :] = heat[i * Y : (i + 1) * Y]

    def leave(u, k):
        some, place = pl.ds(P(u, k), k), pl.ds(B(u, k), k)
        if u >= SHARE:
            remote(final.at[other, some], tracers_out.at[:, place], across)
            arrivals.append(sent[-1])
            remote(final.at[tracers, some], heat_out.at[place], across)
            arrivals.append(sent[-1])
        leaving.append(local(final.at[mine, some], tracers_out.at[:, place]))
        leaving.append(local(final.at[tracers, some], heat_out.at[place]))

    for action in SCHEDULE(half):
        if action[0] == "x":
            arrive(action[1])
        elif action[0] == "z":
            arrive_outer()
        elif action[0] == "go":
            advance(*action[1:])
        else:
            leave(*action[1:])
    with jax.named_scope("leaving"):
        for copy in leaving:
            copy.wait()
    for i, copy in enumerate(arrivals):
        with jax.named_scope(f"arrivals{i}"):
            copy.wait_recv()
    for copy in sent:
        copy.wait_send()


def SCHEDULE(half):
    count = len(pair_plan(half)[1])
    a = FIRST
    b = half - STEPS
    first = [("x", i) for i in range(count)]
    return first + [
        ("go", (0, -2, a + 4)),
        ("go", (1, -1, a + 2)),
        ("go", (2, 0, a)),
        ("out", 0, a),
        ("z",),
        ("go", (0, a + 2, b - a)),
        ("go", (1, a + 1, b - a)),
        ("go", (2, a, b - a)),
        ("out", a, b - a),
        ("go", (0, b + 2, 3)),
        ("go", (1, b + 1, 3)),
        ("go", (2, b, 3)),
        ("out", b, 3),
    ]


def paired(shape, groups, regions, sects):
    return (
        groups == 2 and regions > 1 and regions % 2 == 0 and sects > 1
        and shape[2] == 8 and shape[3] == 128 and shape[1] % 2 == 0 and shape[1] >= 24
        and shape[0] * groups * shape[2] == 128
    )


def pair_call(solute, thermal, eastward, northward, layers, rates, yields, regions, sects):
    own, X, Y, wide = solute.shape
    tracers = own * 2
    half = X // 2
    low, ranges = pair_plan(half)
    columns = half - low + STEPS
    operands = [
        pltpu.with_memory_space_constraint(v, pltpu.HBM)
        for v in (solute, thermal, eastward, northward, layers.T, rates, yields.reshape(1, tracers))
    ]
    hbm = pl.BlockSpec(memory_space=pltpu.HBM)
    free = pl.BlockSpec(memory_space=pl.ANY)
    dma = pltpu.SemaphoreType.DMA
    return pl.pallas_call(
        functools.partial(pair_kernel, regions, sects),
        out_shape=(
            jax.ShapeDtypeStruct(solute.shape, jnp.float32),
            jax.ShapeDtypeStruct(thermal.shape, jnp.float32),
        ),
        in_specs=[hbm] * 7,
        out_specs=(free, free),
        scratch_shapes=[
            pltpu.VMEM((Y, X), jnp.int32),
            pltpu.VMEM((tracers, tracers), jnp.float32),
            pltpu.VMEM((1, tracers), jnp.float32),
            pltpu.VMEM((STEPS, tracers + 4, columns, 2 * Y, wide), jnp.float32),
            pltpu.VMEM((6, columns, 2 * Y, wide), jnp.float32),
            pltpu.VMEM((X, Y, wide), jnp.float32),
            pltpu.VMEM((tracers + 1, columns, Y, wide), jnp.float32),
            dma((SENDS,)),
            dma((SENDS,)),
            dma((LOCALS,)),
        ],
        compiler_params=pltpu.CompilerParams(
            collective_id=0, has_side_effects=True, vmem_limit_bytes=40 << 20
        ),
    )(*operands)


SENDS = 64
LOCALS = 32


def solution(mesh):
    regions, groups, sects = (mesh.shape[a] for a in ("region", "tracer", "sect"))

    def body(solute, thermal, eastward, northward, layers, rates, yields):
        if paired(solute.shape, groups, regions, sects):
            return pair_call(
                solute, thermal, eastward, northward, layers, rates, yields, regions, sects
            )
        own, rows, cols, wide = solute.shape
        tracers = own * groups
        span = rows // groups
        fields = tracers + 1
        flat = (rows * cols, wide)
        free, hbm = pl.BlockSpec(memory_space=pl.ANY), pl.BlockSpec(memory_space=pltpu.HBM)
        dma = pltpu.SemaphoreType.DMA
        peers = max(groups - 1, 1)
        chunks = plan(span)[0]
        mixture, heat = pl.pallas_call(
            functools.partial(kernel, regions, groups, sects),
            out_shape=(
                jax.ShapeDtypeStruct((own, *flat), jnp.float32),
                jax.ShapeDtypeStruct(flat, jnp.float32),
            ),
            in_specs=[hbm] * 7,
            out_specs=(free, free),
            scratch_shapes=[
                pltpu.VMEM((cols, rows), jnp.int32),
                pltpu.VMEM((tracers, tracers), jnp.float32),
                pltpu.VMEM((1, tracers), jnp.float32),
                pltpu.VMEM((STEPS, fields + 3, (span + 2) * cols, wide), jnp.float32),
                pltpu.VMEM((STEPS, chunks, 2, fields + 3, span // chunks, wide), jnp.float32),
                pltpu.VMEM((STEPS, chunks, 2, fields + 3, span // chunks, wide), jnp.float32),
                pltpu.VMEM((6, *flat), jnp.float32),
                pltpu.VMEM((fields, span * cols, wide), jnp.float32),
                dma((peers, chunks)),
                dma((peers, chunks)),
                dma((STEPS, chunks, 4)),
                dma((STEPS, chunks, 4)),
                dma((peers, chunks, 2)),
                dma((peers, chunks, 2)),
                dma((chunks, 3)),
                dma((6,)),
            ],
            compiler_params=pltpu.CompilerParams(
                collective_id=0, has_side_effects=True, vmem_limit_bytes=60 << 20
            ),
        )(
            solute.reshape(own, *flat),
            thermal.reshape(flat),
            eastward.reshape(flat),
            northward.reshape(flat),
            layers.T,
            rates,
            yields.reshape(1, tracers),
        )
        return mixture.reshape(solute.shape), heat.reshape(thermal.shape)

    return jax.shard_map(
        body,
        mesh=mesh,
        in_specs=(
            P("tracer", "region", "sect", None),
            P("region", "sect", None),
            P("region", "sect", None),
            P("region", "sect", None),
            P("region", "sect"),
            P(),
            P(),
        ),
        out_specs=(P("tracer", "region", "sect", None), P("region", "sect", None)),
        check_vma=False,
    )
```

```python
import functools
import math

import jax
import jax.numpy as jnp
from jax import lax
from jax.experimental import pallas as pl
from jax.experimental.pallas import tpu as pltpu
from jax.sharding import PartitionSpec as P

STEPS = 3
SUB = 4

TIME_STEP = 0.2
REACT_STEP = 0.1
GROWTH_MAX = 1.0
HALF_SAT = 0.5
WATER_ATT = 3.0
CHL_ATT = 2.0
HEAT_GAIN = 0.5

MESH = pl.DeviceIdType.MESH
HIGHEST = lax.Precision.HIGHEST
EAST, WEST, NORTH, SOUTH = range(4)


def iota(shape, dim):
    return lax.broadcasted_iota(jnp.int32, shape, dim)


def exact_dot(a, b, dims=((1,), (0,))):
    return lax.dot_general(
        a, b, (dims, ((), ())), precision=HIGHEST, preferred_element_type=jnp.float32
    )


def halves(x):
    high = x.astype(jnp.bfloat16)
    return high, (x - high.astype(jnp.float32)).astype(jnp.bfloat16)


def half_dot(a, b):
    return jnp.dot(a, b, preferred_element_type=jnp.float32)


def dot3(a, b):
    return half_dot(a[0], b[0]) + half_dot(a[1], b[0]) + half_dot(a[0], b[1])


def tables(rates_ref, yields_ref, tracers, wide, Y):
    rows = tracers * Y
    spread = (iota((rows, tracers), 0) // Y == iota((rows, tracers), 1)).astype(jnp.float32)
    same = iota((rows, rows), 0) % Y == iota((rows, rows), 1) % Y
    full = exact_dot(exact_dot(spread, rates_ref[...]), spread, ((1,), (1,)))
    full = jnp.where(same, full, 0.0) * REACT_STEP
    diagonal = (iota((rows, rows), 0) == iota((rows, rows), 1)).astype(jnp.float32)
    one = diagonal + full
    two = exact_dot(one, one)
    three = exact_dot(two, one)
    four = exact_dot(two, two)
    source = [
        exact_dot(spread * yields_ref[...], jnp.ones((tracers, wide), jnp.float32)) * REACT_STEP
    ]
    for power in (one, two, three):
        source.append(exact_dot(power, source[0]))
    head = jnp.concatenate([power[: 3 * Y] for power in (one, two, three)], axis=0)
    shape = (rows, wide)
    lane = iota(shape, 1)
    inject = jnp.zeros(shape, jnp.float32)
    for sub in range(SUB):
        hit = jnp.logical_and(lane // Y == sub, lane % Y == iota(shape, 0) % Y)
        inject = inject + jnp.where(hit, source[SUB - 1 - sub], 0.0)
    return head, four, inject[:, : SUB * Y], [v[: 3 * Y] for v in source[: SUB - 1]]


def stack(flat, wide):
    return jnp.concatenate(
        [flat[:, i * wide : (i + 1) * wide] for i in range(flat.shape[1] // wide)], axis=0
    )


def unstack(tall, Y):
    return jnp.concatenate(
        [tall[i * Y : (i + 1) * Y] for i in range(tall.shape[0] // Y)], axis=1
    )


def plan(span):
    return (3, (0, 2, 1)) if span % 3 == 0 else (1, (0,))


def kernel(
    regions, groups, sects,
    solute, heat_hbm, east_hbm, north_hbm, layers_hbm, rates_hbm, yields_hbm,
    tracers_out, heat_out,
    layers_in, rates_ref, yields_ref,
    state, ysend, yrecv, coef, final,
    in_send, in_recv, halo_send, halo_recv, out_send, out_recv, local_sem, load_sem,
):
    region, group, sect = (lax.axis_index(a) for a in ("region", "tracer", "sect"))
    own, wide, Y = solute.shape[0], solute.shape[2], layers_in.shape[0]
    tracers = own * groups
    block = heat_hbm.shape[0] // groups
    span = block // Y
    fields = tracers + 1
    every = fields + 3

    def place(reg, t):
        return t + (reg % 2) * (groups - 1 - 2 * t)

    part = place(region, group)
    last = groups - 1
    next_region = lax.rem(region + 1, regions)
    past_region = lax.rem(region + regions - 1, regions)
    east_region = jnp.where(part == last, next_region, region)
    west_region = jnp.where(part == 0, past_region, region)
    east_part = jnp.where(part == last, 0, part + 1)
    west_part = jnp.where(part == 0, last, part - 1)
    beside = {
        EAST: {"region": east_region, "tracer": place(east_region, east_part)},
        WEST: {"region": west_region, "tracer": place(west_region, west_part)},
        NORTH: {"sect": lax.rem(sect + 1, sects)},
        SOUTH: {"sect": lax.rem(sect + sects - 1, sects)},
    }
    peers = [lax.rem(group + d, groups) for d in range(1, groups)]

    def rows_of(t):
        return pl.ds(pl.multiple_of(place(region, t) * block, Y), block)

    mine = rows_of(group)
    slot = pl.ds(group * own, own)
    inner = pl.ds(Y, block)

    barrier = pltpu.get_barrier_semaphore()
    for peer in peers:
        pl.semaphore_signal(barrier, inc=1, device_id={"tracer": peer}, device_id_type=MESH)
    for side in range(4):
        pl.semaphore_signal(barrier, inc=1, device_id=beside[side], device_id_type=MESH)
    keep = pltpu.make_async_copy(
        solute.at[:, mine, :], state.at[0, slot, inner, :], local_sem.at[0, 0]
    )
    keep.start()
    loads = []
    for i, (source_ref, target_ref) in enumerate(
        (
            (layers_hbm, layers_in),
            (rates_hbm, rates_ref),
            (yields_hbm, yields_ref),
            (heat_hbm.at[mine, :], state.at[0, tracers, inner, :]),
            (east_hbm.at[mine, :], state.at[0, fields, inner, :]),
            (north_hbm.at[mine, :], state.at[0, fields + 1, inner, :]),
        )
    ):
        copy = pltpu.make_async_copy(source_ref, target_ref, load_sem.at[i])
        copy.start()
        loads.append(copy)
    pl.semaphore_wait(barrier, groups - 1 + 4)

    chunks, order = plan(span)
    deep = span // chunks
    piece = deep * Y

    def part_of(t, c):
        return pl.ds(pl.multiple_of(place(region, t) * block + c * piece, Y), piece)

    arriving = {}
    for i, c in enumerate(order):
        for d, peer in enumerate(peers):
            copy = pltpu.make_async_remote_copy(
                src_ref=solute.at[:, part_of(peer, c), :],
                dst_ref=state.at[0, slot, pl.ds(Y + c * piece, piece), :],
                send_sem=in_send.at[d, c],
                recv_sem=in_recv.at[d, c],
                device_id={"tracer": peer},
                device_id_type=MESH,
            )
            copy.start()
            arriving[c, d] = copy

    for copy in loads:
        copy.wait()
    total = layers_in.shape[1] * Y
    pick = (iota((total, layers_in.shape[1]), 0) // Y == iota((total, layers_in.shape[1]), 1))
    depth = lax.dot_general(
        pick.astype(jnp.bfloat16),
        layers_in[...].astype(jnp.float32).astype(jnp.bfloat16),
        (((1,), (1,)), ((), ())),
        preferred_element_type=jnp.float32,
    )
    depth = jnp.where(iota((total, Y), 0) % Y == iota((total, Y), 1), depth, 0.0)
    depth = half_dot(depth.astype(jnp.bfloat16), jnp.ones((Y, wide), jnp.bfloat16))
    coef[5] = (iota((total, wide), 1).astype(jnp.float32) < depth).astype(jnp.float32)
    state[0, fields + 2, inner, :] = coef[5, mine, :]

    head, four, inject, source = tables(rates_ref, yields_ref, tracers, wide, Y)
    head, four, inject = halves(head), halves(four), halves(inject)
    upper = (iota((wide, wide), 0) < iota((wide, wide), 1)).astype(jnp.bfloat16)
    level = iota((piece, wide), 1).astype(jnp.float32) + 0.5
    tile = (1, deep)
    source = [jnp.tile(v, tile) for v in source]

    def light(chl_abs):
        high, low = halves(chl_abs)
        above = half_dot(high, upper) + half_dot(low, upper)
        return jnp.exp(
            -(WATER_ATT / wide * level + CHL_ATT / wide * (above + 0.5 * chl_abs))
        )

    sent = []

    def exchange(step, c):
        count = every if step == 0 else fields
        some = pl.ds(0, count)
        moves = {}
        if c == chunks - 1:
            moves[EAST] = (
                state.at[step, some, pl.ds(block, Y), :],
                state.at[step, some, pl.ds(0, Y), :],
            )
        if c == 0:
            moves[WEST] = (
                state.at[step, some, pl.ds(Y, Y), :],
                state.at[step, some, pl.ds(block + Y, Y), :],
            )

        def send(moves):
            for side, (source_ref, target_ref) in moves.items():
                copy = pltpu.make_async_remote_copy(
                    src_ref=source_ref,
                    dst_ref=target_ref,
                    send_sem=halo_send.at[step, c, side],
                    recv_sem=halo_recv.at[step, c, side],
                    device_id=beside[side],
                    device_id_type=MESH,
                )
                copy.start()
                sent.append(copy)
                halos[step, c, side] = copy

        send(moves)
        for f in range(count):
            for side, y in ((0, 0), (1, Y - 1)):
                ysend[step, c, side, f] = state[
                    step, f, pl.ds(Y + c * piece + y, deep, stride=Y), :
                ]
        moves = {
            NORTH: (ysend.at[step, c, 1, some], yrecv.at[step, c, 1, some]),
            SOUTH: (ysend.at[step, c, 0, some], yrecv.at[step, c, 0, some]),
        }
        send(moves)

    halos = {}

    def beside_y(step, value, x, first, count):
        at = (count, Y, wide)
        row = iota(at, 1)
        some = pl.ds(first, count)
        above = jnp.broadcast_to(yrecv[step, x // deep, 0, some, pl.ds(x % deep, 1), :], at)
        below = jnp.broadcast_to(yrecv[step, x // deep, 1, some, pl.ds(x % deep, 1), :], at)
        up = jnp.where(row == Y - 1, above, pltpu.roll(value, Y - 1, 1))
        down = jnp.where(row == 0, below, pltpu.roll(value, 1, 1))
        return up, down

    keep.wait()
    for c in order:
        for d in range(len(peers)):
            arriving[c, d].wait_recv()
        exchange(0, c)

    leaving = []

    def leave(c):
        rows = pl.ds(c * piece, piece)
        out_rows = part_of(group, c)
        for d, peer in enumerate(peers):
            pairs = (
                (final.at[pl.ds(peer * own, own), rows, :], tracers_out.at[:, out_rows, :]),
                (final.at[tracers, rows, :], heat_out.at[out_rows, :]),
            )
            for i, (source_ref, target_ref) in enumerate(pairs):
                copy = pltpu.make_async_remote_copy(
                    src_ref=source_ref,
                    dst_ref=target_ref,
                    send_sem=out_send.at[d, c, i],
                    recv_sem=out_recv.at[d, c, i],
                    device_id={"tracer": peer},
                    device_id_type=MESH,
                )
                copy.start()
                leaving.append(copy)
        pairs = (
            (final.at[slot, rows, :], tracers_out.at[:, out_rows, :]),
            (final.at[tracers, rows, :], heat_out.at[out_rows, :]),
        )
        for i, (source_ref, target_ref) in enumerate(pairs):
            copy = pltpu.make_async_copy(source_ref, target_ref, local_sem.at[c, 1 + i])
            copy.start()
            leaving.append(copy)

    def advance(step, c):
        columns, heats, wets = [], [], []
        for x in range(c * deep, (c + 1) * deep):
            here = pl.ds((x + 1) * Y, Y)
            ahead = pl.ds((x + 2) * Y, Y)
            behind = pl.ds(x * Y, Y)
            cell = pl.ds(x * Y, Y)
            if step == 0:
                speed_wet = state[0, pl.ds(fields + 1, 2), here, :]
                up, down = beside_y(0, speed_wet, x, fields + 1, 2)
                wet = speed_wet[1]
                east = state[0, fields, here, :] * wet * state[0, fields + 2, ahead, :]
                west = state[0, fields, behind, :] * state[0, fields + 2, behind, :] * wet
                north = speed_wet[0] * wet * up[1]
                south = down[0] * down[1] * wet
                scaled = TIME_STEP * wet
                coef[0, cell, :] = wet - scaled * (
                    jnp.maximum(east, 0.0) - jnp.minimum(west, 0.0)
                    + jnp.maximum(north, 0.0) - jnp.minimum(south, 0.0)
                )
                coef[1, cell, :] = -scaled * jnp.minimum(east, 0.0)
                coef[2, cell, :] = scaled * jnp.maximum(west, 0.0)
                coef[3, cell, :] = -scaled * jnp.minimum(north, 0.0)
                coef[4, cell, :] = scaled * jnp.maximum(south, 0.0)
            value = state[step, pl.ds(0, fields), here, :]
            up, down = beside_y(step, value, x, 0, fields)
            moved = (
                coef[0, cell, :] * value
                + coef[1, cell, :] * state[step, pl.ds(0, fields), ahead, :]
                + coef[2, cell, :] * state[step, pl.ds(0, fields), behind, :]
                + coef[3, cell, :] * up
                + coef[4, cell, :] * down
            )
            columns.append(moved[:tracers].reshape(tracers * Y, wide))
            heats.append(moved[tracers])
            wets.append(state[0, fields + 2, here, :])
        mixed = jnp.concatenate(columns, axis=1)
        parts = halves(mixed)
        ahead_rows = dot3(head, parts)
        result = dot3(four, parts)
        rates = []
        for sub in range(SUB):
            if sub == 0:
                rows = mixed[: 3 * Y]
            else:
                rows = ahead_rows[(sub - 1) * 3 * Y : sub * 3 * Y]
                for i, rate in enumerate(rates):
                    rows = rows + source[sub - 1 - i] * jnp.concatenate([rate] * 3, axis=0)
            nutrient, chl, phyto = rows[:Y], rows[Y : 2 * Y], rows[2 * Y :]
            shade = unstack(light(jnp.abs(stack(chl, wide))), Y)
            rates.append(
                GROWTH_MAX * shade * nutrient / (jnp.abs(nutrient) + HALF_SAT) * phyto
            )
        result = result + dot3(inject, halves(jnp.concatenate(rates, axis=0)))
        chl_abs = jnp.abs(stack(result[Y : 2 * Y], wide))
        heating = HEAT_GAIN * chl_abs * light(chl_abs)
        heat = jnp.concatenate(heats, axis=0) + TIME_STEP * jnp.concatenate(wets, axis=0) * heating
        if step < STEPS - 1:
            target, base = state.at[step + 1], Y + c * piece
        else:
            target, base = final, c * piece
        for x in range(deep):
            target[pl.ds(0, tracers), pl.ds(base + x * Y, Y), :] = result[
                :, x * wide : (x + 1) * wide
            ].reshape(tracers, Y, wide)
        target[tracers, pl.ds(base, piece), :] = heat

    for step in range(STEPS):
        for c in order:
            for side in (NORTH, SOUTH):
                halos[step, c, side].wait_recv()
            if c == 0:
                halos[step, chunks - 1, EAST].wait_recv()
            if c == chunks - 1:
                halos[step, 0, WEST].wait_recv()
            advance(step, c)
            if step < STEPS - 1:
                exchange(step + 1, c)
            else:
                leave(c)
    for copy in leaving:
        copy.wait()
    for copy in sent + list(arriving.values()):
        copy.wait_send()

SHARE = 3
FIRST = 3


def wide_halves(x):
    high, low = halves(x)
    return jnp.concatenate([high, high, low], axis=1)


def tall_halves(x):
    high, low = halves(x)
    return jnp.concatenate([high, low, high], axis=0)


def pair_tables(rates_ref, yields_ref, tracers, wide, Y):
    rows = tracers * Y
    spread = (iota((rows, tracers), 0) // Y == iota((rows, tracers), 1)).astype(jnp.float32)
    same = iota((rows, rows), 0) % Y == iota((rows, rows), 1) % Y
    full = exact_dot(exact_dot(spread, rates_ref[...]), spread, ((1,), (1,)))
    full = jnp.where(same, full, 0.0) * REACT_STEP
    diagonal = (iota((rows, rows), 0) == iota((rows, rows), 1)).astype(jnp.float32)
    one = diagonal + full
    two = exact_dot(one, one)
    three = exact_dot(two, one)
    four = exact_dot(two, two)
    source = [
        exact_dot(spread * yields_ref[...], jnp.ones((tracers, wide), jnp.float32)) * REACT_STEP
    ]
    for power in (one, two, three):
        source.append(exact_dot(power, source[0]))
    powers = jnp.concatenate([power[: 3 * Y] for power in (one, two, three)] + [four], axis=0)
    shape = (rows, wide)
    lane = iota(shape, 1)
    inject = jnp.zeros(shape, jnp.float32)
    for sub in range(SUB):
        hit = jnp.logical_and(lane // Y == sub, lane % Y == iota(shape, 0) % Y)
        inject = inject + jnp.where(hit, source[SUB - 1 - sub], 0.0)
    return (
        wide_halves(powers),
        wide_halves(inject[:, : SUB * Y]),
        [v[: 3 * Y] for v in source],
    )


def pair_plan(half):
    low = -SHARE - STEPS
    ranges = [(half - STEPS, STEPS)]
    for at, end in ((SHARE - STEPS, half - STEPS), (low, SHARE - STEPS)):
        while at < end:
            size = min(STEPS, end - at)
            ranges.append((at, size))
            at += size
    return low, ranges


def pair_kernel(
    regions, sects,
    solute, heat_hbm, east_hbm, north_hbm, layers_hbm, rates_hbm, yields_hbm,
    tracers_out, heat_out,
    layers_in, rates_ref, yields_ref, state, coef, wets, final, measure,
    send_sem, recv_sem,
):
    groups = 2
    region, group, sect = (lax.axis_index(a) for a in ("region", "tracer", "sect"))
    own, X, Y, wide = solute.shape
    half = X // groups
    tracers = own * groups
    fields = tracers + 1
    base = STEPS + 1
    low, ranges = pair_plan(half)
    reach = half - low
    odd = region % 2
    part = group + odd * (1 - 2 * group)
    peer = 1 - group

    def pick(flag, a, b):
        return a + flag * (b - a)

    def P(u, k, flag=part):
        return pick(flag, half + STEPS - u - k, u - low)

    def B(u, k, flag=part):
        return pick(flag, half - u - k, half + u)

    outer_region = lax.rem(region + pick(part, regions - 1, 1), regions)
    outer_part = 1 - part
    outer_odd = outer_region % 2
    beside = {"region": outer_region, "tracer": outer_part + outer_odd * (1 - 2 * outer_part)}
    north = {"sect": lax.rem(sect + 1, sects)}
    south = {"sect": lax.rem(sect + sects - 1, sects)}
    across = {"tracer": peer}
    mine, other = pl.ds(group * own, own), pl.ds(peer * own, own)

    names, lines = {}, {}

    def slot(name):
        return names.setdefault(name, len(names))

    def tally(name, ref):
        lines[name] = lines.get(name, 0) + math.prod(ref.shape) // wide

    def settle(name, sems=recv_sem):
        some = measure.at[pl.ds(0, lines[name])]
        at = slot(name) if sems is recv_sem else int(name[4:])
        with jax.named_scope(name):
            pltpu.make_async_copy(some, some, sems.at[at]).wait()

    def local(name, source_ref, target_ref):
        tally(name, target_ref)
        pltpu.make_async_copy(source_ref, target_ref, recv_sem.at[slot(name)]).start()

    def remote(name, source_ref, target_ref, device, turn=0):
        tally(name, target_ref)
        tally(f"sent{turn}", source_ref)
        push(name, source_ref, target_ref, device, turn)

    def push(name, source_ref, target_ref, device, turn=0):
        pltpu.make_async_remote_copy(
            src_ref=source_ref,
            dst_ref=target_ref,
            send_sem=send_sem.at[turn],
            recv_sem=recv_sem.at[slot(name)],
            device_id=device,
            device_id_type=MESH,
        ).start()

    raw = state.at[0]
    body = pl.ds(base, Y)
    blank = jnp.zeros((tracers + 4, 1, STEPS, wide), jnp.float32)
    for u in (low, half, half + 1, half + 2):
        for row in (base - STEPS, base + Y):
            raw[:, pl.ds(P(u, 1), 1), pl.ds(row, STEPS), :] = blank
    barrier = pltpu.get_barrier_semaphore()
    for device in (across, beside, north, south):
        pl.semaphore_signal(barrier, inc=1, device_id=device, device_id_type=MESH)

    small = [
        pltpu.make_async_copy(source_ref, target_ref, recv_sem.at[slot(f"small{i}")])
        for i, (source_ref, target_ref) in enumerate(
            ((layers_hbm, layers_in), (rates_hbm, rates_ref), (yields_hbm, yields_ref))
        )
    ]
    for copy in small:
        copy.start()
    p_all, b_all = P(low, reach), B(low, reach)
    in_block = pl.ds(b_all, reach)
    in_state = pl.ds(p_all, reach)
    extra = ((heat_hbm, tracers), (east_hbm, fields), (north_hbm, fields + 1))
    local("loads", solute.at[:, in_block], raw.at[mine, in_state, body])
    for ref, field in extra:
        local("loads", ref.at[in_block], raw.at[field, in_state, body])

    with jax.named_scope("barrier"):
        pl.semaphore_wait(barrier, 4)

    def cross(i):
        u, k = ranges[i]
        remote(
            f"x{i}",
            solute.at[:, pl.ds(B(u, k, 1 - part), k)],
            raw.at[mine, pl.ds(P(u, k, 1 - part), k), body],
            across,
        )

    edge = half - STEPS
    edge_block = pl.ds(B(edge, STEPS), STEPS)
    edge_state = pl.ds(P(edge, STEPS), STEPS)
    past = pl.ds(pick(part, reach, 0), STEPS)
    cross(0)
    remote("outer", solute.at[:, edge_block], raw.at[mine, past, body], beside)
    for ref, field in extra:
        remote("outer", ref.at[edge_block], raw.at[field, past, body], beside)
    for i in range(1, len(ranges)):
        cross(i)
    far = sect % 2

    def both_sides(send):
        for first in (0, 1):
            @pl.when(far == first)
            def _():
                for side in (first, 1 - first):
                    send(side, (south, north)[side])

    def halo_row(side, deep=STEPS):
        return pl.ds(base - deep if side else base + Y, deep)

    def tally_sides(name, refs):
        for ref in refs:
            for _ in range(2):
                tally(name, ref)
                tally("sent0", ref)

    def direct_rows(name, u, k):
        b, p = pl.ds(B(u, k), k), pl.ds(P(u, k), k)
        refs = [(solute.at[:, b], mine)] + [(ref.at[b], field) for ref, field in extra]

        def send(side, device):
            block_rows = pl.ds(Y - STEPS if side else 0, STEPS)
            for ref, field in refs:
                rows = ref.at[:, :, block_rows] if ref is refs[0][0] else ref.at[:, block_rows]
                push(name, rows, raw.at[field, p, halo_row(side)], device)

        both_sides(send)
        tally_sides(name, [raw.at[field, p, halo_row(0)] for _, field in refs])

    def beside_rows(name, some, u, k, deep=STEPS):
        place = pl.ds(P(u, k), k)

        def send(side, device):
            start = base + Y - deep if side else base
            push(
                name,
                raw.at[some, place, pl.ds(start, deep)],
                raw.at[some, place, halo_row(side, deep)],
                device,
            )

        both_sides(send)
        tally_sides(name, [raw.at[some, place, halo_row(0, deep)]])

    near = 1 + -(-(FIRST + 2 * STEPS) // STEPS)
    cone = min((near - 1) * STEPS, edge + STEPS + STEPS - SHARE)
    cone_at = max(low + 1, SHARE - STEPS)
    cone_end = SHARE - STEPS + cone
    direct_rows("rows", cone_at, cone_end - cone_at)

    for copy in small:
        copy.wait()
    total = X * Y
    pick_rows = iota((total, X), 0) // Y == iota((total, X), 1)
    depth = lax.dot_general(
        pick_rows.astype(jnp.bfloat16),
        layers_in[...].astype(jnp.float32).astype(jnp.bfloat16),
        (((1,), (1,)), ((), ())),
        preferred_element_type=jnp.float32,
    )
    depth = jnp.where(iota((total, Y), 0) % Y == iota((total, Y), 1), depth, 0.0)
    depth = half_dot(depth.astype(jnp.bfloat16), jnp.ones((Y, wide), jnp.bfloat16))
    wets[...] = (iota((total, wide), 1).astype(jnp.float32) < depth).astype(jnp.float32).reshape(
        X, Y, wide
    )
    wet_field = fields + 2
    raw[wet_field, in_state, body, :] = wets[in_block]
    remote("outer", raw.at[wet_field, edge_state, body], raw.at[wet_field, past, body], beside)
    beside_rows("rows", pl.ds(wet_field, 1), low + 1, reach - 1)

    with jax.named_scope("make_tables"):
        powers, inject, source = pair_tables(rates_ref, yields_ref, tracers, wide, Y)
    shape = (wide, wide)
    upper = (iota(shape, 0) < iota(shape, 1)).astype(jnp.float32)
    upper = upper + 0.5 * (iota(shape, 0) == iota(shape, 1)).astype(jnp.float32)
    upper = jnp.concatenate([upper.astype(jnp.bfloat16)] * 2, axis=0)
    level = (iota((Y, wide), 1).astype(jnp.float32) + 0.5) * (-WATER_ATT / wide)
    settle("loads")

    def light(chl_abs):
        high, low_part = halves(chl_abs)
        above = half_dot(jnp.concatenate([high, low_part], axis=1), upper)
        tall = jnp.concatenate([level] * (chl_abs.shape[0] // Y), axis=0)
        return jnp.exp(tall - CHL_ATT / wide * above)

    done = set()

    def once(name):
        fresh = name not in done
        done.add(name)
        return fresh

    def arrive(i):
        if once(f"x{i}"):
            settle(f"x{i}")
            u, k = ranges[i]
            some = pl.ds(P(u, k), k)
            if i == 0:
                remote("outer", raw.at[other, some, body], raw.at[other, past, body], beside)
            skip = int(u == low)
            beside_rows(f"y{i}", other, u + skip, k - skip)
            if i == near - 1:
                if cone_end < half:
                    direct_rows("rest", cone_end, half - cone_end)
                if low + 1 < cone_at:
                    direct_rows("rest", low + 1, cone_at - low - 1)

    def arrive_outer():
        arrive(0)
        if once("outer"):
            settle("outer")
            beside_rows("corner", slice(None), half, STEPS - 1, STEPS - 1)

    def ready(first, last):
        if once("rows"):
            settle("rows")
        if (first < cone_at - 1 or last >= cone_end) and "rest" in lines and once("rest"):
            settle("rest")
        for i, (u, k) in enumerate(ranges):
            if u <= last and first < u + k:
                arrive(i)
                if once(f"y{i}"):
                    settle(f"y{i}")
        if last >= half:
            arrive_outer()
            if once("corner"):
                settle("corner")

    windows = [
        (base - STEPS + 1, base + Y + STEPS - 1 - Y),
        (base - 1, base + 1),
        (base,),
    ]

    def stencil(step, p, r):
        here = pl.ds(r, Y)
        up_rows, down_rows = pl.ds(r + 1, Y), pl.ds(r - 1, Y)
        if step == 0:
            wet = raw[wet_field, p, here, :]
            south_wet = raw[wet_field, p, down_rows, :]
            east = raw[fields, p, here, :] * wet * raw[wet_field, p + 1, here, :]
            west = raw[fields, p - 1, here, :] * raw[wet_field, p - 1, here, :] * wet
            up = raw[fields + 1, p, here, :] * wet * raw[wet_field, p, up_rows, :]
            down = raw[fields + 1, p, down_rows, :] * south_wet * wet
            scaled = TIME_STEP * wet
            c = [
                wet
                - scaled
                * (
                    jnp.maximum(east, 0.0) - jnp.minimum(west, 0.0)
                    + jnp.maximum(up, 0.0) - jnp.minimum(down, 0.0)
                ),
                -scaled * jnp.minimum(east, 0.0),
                scaled * jnp.maximum(west, 0.0),
                -scaled * jnp.minimum(up, 0.0),
                scaled * jnp.maximum(down, 0.0),
                scaled,
            ]
            for i, v in enumerate(c):
                coef[i, p, here, :] = v
        else:
            c = [coef[i, p, here, :] for i in range(6)]
        some = pl.ds(0, fields)
        moved = (
            c[0] * state[step, some, p, here, :]
            + c[1] * state[step, some, p + 1, here, :]
            + c[2] * state[step, some, p - 1, here, :]
            + c[3] * state[step, some, p, up_rows, :]
            + c[4] * state[step, some, p, down_rows, :]
        )
        return moved, c[5]

    def advance(*work):
        for step, u, k in work:
            if step == 0:
                ready(u - 1, u + k)
        with jax.named_scope("go" + "_".join(f"{s}:{u}:{k}" for s, u, k in work)):
            compute(work)

    def compute(work):
        tiles = []
        for step, u, k in work:
            p = P(u, k)
            for i in range(k):
                for r in windows[step]:
                    tiles.append((step, p + i, r))
        columns, heats, scales = [], [], []
        for step, p, r in tiles:
            moved, scaled = stencil(step, p, r)
            columns.append(moved[:tracers].reshape(tracers * Y, wide))
            heats.append(moved[tracers])
            scales.append(scaled)
        n = len(tiles)
        mixed = jnp.concatenate(columns, axis=1)
        ahead = half_dot(powers, tall_halves(mixed))
        block = 3 * Y
        result = ahead[3 * block :]

        def part_of(rows, i):
            return stack(rows[i * Y : (i + 1) * Y], wide)

        def spread(v, i):
            return jnp.concatenate([v[i * Y : (i + 1) * Y]] * n, axis=0)

        rates = []
        for sub in range(SUB):
            rows = mixed[:block] if sub == 0 else ahead[(sub - 1) * block : sub * block]
            value = []
            for i in range(3):
                v = part_of(rows, i)
                for j, rate in enumerate(rates):
                    v = v + spread(source[sub - 1 - j], i) * rate
                value.append(v)
            nutrient, chl, phyto = value
            rates.append(
                light(jnp.abs(chl)) * (nutrient / (jnp.abs(nutrient) + HALF_SAT) * phyto)
            )
        chl = part_of(result, 1)
        for j, rate in enumerate(rates):
            chl = chl + spread(source[SUB - 1 - j], 1) * rate
        chl_abs = jnp.abs(chl)
        flat = jnp.concatenate([unstack(rate, Y) for rate in rates], axis=0)
        result = result + half_dot(inject, tall_halves(flat))
        heat = jnp.concatenate(heats, axis=0) + HEAT_GAIN * (
            jnp.concatenate(scales, axis=0) * chl_abs * light(chl_abs)
        )
        for i, (step, p, r) in enumerate(tiles):
            value = result[:, i * wide : (i + 1) * wide].reshape(tracers, Y, wide)
            if step < STEPS - 1:
                here = pl.ds(r, Y)
                state[step + 1, pl.ds(0, tracers), p, here, :] = value
                state[step + 1, tracers, p, here, :] = heat[i * Y : (i + 1) * Y]
            else:
                final[pl.ds(0, tracers), p, :, :] = value
                final[tracers, p, :, :] = heat[i * Y : (i + 1) * Y]

    def leave(u, k):
        some, place = pl.ds(P(u, k), k), pl.ds(B(u, k), k)
        if u >= SHARE:
            remote("arrivals", final.at[other, some], tracers_out.at[:, place], across, 1)
            remote("arrivals", final.at[tracers, some], heat_out.at[place], across, 1)
        local("leaving", final.at[mine, some], tracers_out.at[:, place])
        local("leaving", final.at[tracers, some], heat_out.at[place])

    for action in schedule(half):
        if action[0] == "x":
            arrive(action[1])
        elif action[0] == "z":
            arrive_outer()
        elif action[0] == "go":
            advance(*action[1:])
        else:
            leave(*action[1:])
    settle("leaving")
    settle("arrivals")
    settle("sent0", send_sem)
    settle("sent1", send_sem)


def schedule(half):
    count = len(pair_plan(half)[1])
    h, a, b = SHARE, FIRST, half - STEPS
    near = 1 + -(-(a + 2 * STEPS) // STEPS)
    inner = [[(s, -h - 2 + s, 2 * h)] if h else [] for s in range(STEPS)]
    own = 1 + -(-(b - h + STEPS) // STEPS)
    rest = half - h - a
    plan = [("x", i) for i in range(own)]
    plan += [("z",), ("go", (0, h - 2, a + 4)), ("go", (1, h - 1, a + 2))]
    plan += [("x", i) for i in range(own, count)]
    plan += [
        ("go", (2, h, a), (0, h + a + 2, rest)),
        ("out", h, a),
        ("go", (1, h + a + 1, rest)),
        ("go", (2, h + a, rest)),
        ("out", h + a, rest),
    ]
    for s in range(STEPS if h else 0):
        plan.append(("go", *inner[s]))
    return plan + ([("out", -h, 2 * h)] if h else [])


def paired(shape, groups, regions, sects):
    return (
        groups == 2 and regions > 1 and regions % 2 == 0 and sects > 1
        and shape[2] == 8 and shape[3] == 128 and shape[1] % 2 == 0 and shape[1] >= 24
        and shape[0] * groups * shape[2] == 128
    )


def pair_call(solute, thermal, eastward, northward, layers, rates, yields, regions, sects):
    own, X, Y, wide = solute.shape
    tracers = own * 2
    half = X // 2
    low, ranges = pair_plan(half)
    columns = half - low + STEPS
    operands = [
        pltpu.with_memory_space_constraint(v, pltpu.HBM)
        for v in (solute, thermal, eastward, northward, layers.T, rates, yields.reshape(1, tracers))
    ]
    hbm = pl.BlockSpec(memory_space=pltpu.HBM)
    free = pl.BlockSpec(memory_space=pl.ANY)
    dma = pltpu.SemaphoreType.DMA
    return pl.pallas_call(
        functools.partial(pair_kernel, regions, sects),
        out_shape=(
            jax.ShapeDtypeStruct(solute.shape, jnp.float32),
            jax.ShapeDtypeStruct(thermal.shape, jnp.float32),
        ),
        in_specs=[hbm] * 7,
        out_specs=(free, free),
        scratch_shapes=[
            pltpu.VMEM((Y, X), jnp.int32),
            pltpu.VMEM((tracers, tracers), jnp.float32),
            pltpu.VMEM((1, tracers), jnp.float32),
            pltpu.VMEM((STEPS, tracers + 4, columns, 2 * Y, wide), jnp.float32),
            pltpu.VMEM((6, columns, 2 * Y, wide), jnp.float32),
            pltpu.VMEM((X, Y, wide), jnp.float32),
            pltpu.VMEM((tracers + 1, columns, Y, wide), jnp.float32),
            pltpu.VMEM((MEASURE, wide), jnp.float32),
            dma((2,)),
            dma((len(ranges) * 2 + 10,)),
        ],
        compiler_params=pltpu.CompilerParams(
            collective_id=0, has_side_effects=True, vmem_limit_bytes=40 << 20
        ),
    )(*operands)


MEASURE = 8192


def solution(mesh):
    regions, groups, sects = (mesh.shape[a] for a in ("region", "tracer", "sect"))

    def body(solute, thermal, eastward, northward, layers, rates, yields):
        if paired(solute.shape, groups, regions, sects):
            return pair_call(
                solute, thermal, eastward, northward, layers, rates, yields, regions, sects
            )
        own, rows, cols, wide = solute.shape
        tracers = own * groups
        span = rows // groups
        fields = tracers + 1
        flat = (rows * cols, wide)
        free, hbm = pl.BlockSpec(memory_space=pl.ANY), pl.BlockSpec(memory_space=pltpu.HBM)
        dma = pltpu.SemaphoreType.DMA
        peers = max(groups - 1, 1)
        chunks = plan(span)[0]
        mixture, heat = pl.pallas_call(
            functools.partial(kernel, regions, groups, sects),
            out_shape=(
                jax.ShapeDtypeStruct((own, *flat), jnp.float32),
                jax.ShapeDtypeStruct(flat, jnp.float32),
            ),
            in_specs=[hbm] * 7,
            out_specs=(free, free),
            scratch_shapes=[
                pltpu.VMEM((cols, rows), jnp.int32),
                pltpu.VMEM((tracers, tracers), jnp.float32),
                pltpu.VMEM((1, tracers), jnp.float32),
                pltpu.VMEM((STEPS, fields + 3, (span + 2) * cols, wide), jnp.float32),
                pltpu.VMEM((STEPS, chunks, 2, fields + 3, span // chunks, wide), jnp.float32),
                pltpu.VMEM((STEPS, chunks, 2, fields + 3, span // chunks, wide), jnp.float32),
                pltpu.VMEM((6, *flat), jnp.float32),
                pltpu.VMEM((fields, span * cols, wide), jnp.float32),
                dma((peers, chunks)),
                dma((peers, chunks)),
                dma((STEPS, chunks, 4)),
                dma((STEPS, chunks, 4)),
                dma((peers, chunks, 2)),
                dma((peers, chunks, 2)),
                dma((chunks, 3)),
                dma((6,)),
            ],
            compiler_params=pltpu.CompilerParams(
                collective_id=0, has_side_effects=True, vmem_limit_bytes=60 << 20
            ),
        )(
            solute.reshape(own, *flat),
            thermal.reshape(flat),
            eastward.reshape(flat),
            northward.reshape(flat),
            layers.T,
            rates,
            yields.reshape(1, tracers),
        )
        return mixture.reshape(solute.shape), heat.reshape(thermal.shape)

    return jax.shard_map(
        body,
        mesh=mesh,
        in_specs=(
            P("tracer", "region", "sect", None),
            P("region", "sect", None),
            P("region", "sect", None),
            P("region", "sect", None),
            P("region", "sect"),
            P(),
            P(),
        ),
        out_specs=(P("tracer", "region", "sect", None), P("region", "sect", None)),
        check_vma=False,
    )
```

```python
import functools
import math

import jax
import jax.numpy as jnp
from jax import lax
from jax.experimental import pallas as pl
from jax.experimental.pallas import tpu as pltpu
from jax.sharding import PartitionSpec as P

STEPS = 3
SUB = 4

TIME_STEP = 0.2
REACT_STEP = 0.1
GROWTH_MAX = 1.0
HALF_SAT = 0.5
WATER_ATT = 3.0
CHL_ATT = 2.0
HEAT_GAIN = 0.5

MESH = pl.DeviceIdType.MESH
HIGHEST = lax.Precision.HIGHEST
EAST, WEST, NORTH, SOUTH = range(4)


def iota(shape, dim):
    return lax.broadcasted_iota(jnp.int32, shape, dim)


def exact_dot(a, b, dims=((1,), (0,))):
    return lax.dot_general(
        a, b, (dims, ((), ())), precision=HIGHEST, preferred_element_type=jnp.float32
    )


def halves(x):
    high = x.astype(jnp.bfloat16)
    return high, (x - high.astype(jnp.float32)).astype(jnp.bfloat16)


def half_dot(a, b):
    return jnp.dot(a, b, preferred_element_type=jnp.float32)


def dot3(a, b):
    return half_dot(a[0], b[0]) + half_dot(a[1], b[0]) + half_dot(a[0], b[1])


def tables(rates_ref, yields_ref, tracers, wide, Y):
    rows = tracers * Y
    spread = (iota((rows, tracers), 0) // Y == iota((rows, tracers), 1)).astype(jnp.float32)
    same = iota((rows, rows), 0) % Y == iota((rows, rows), 1) % Y
    full = exact_dot(exact_dot(spread, rates_ref[...]), spread, ((1,), (1,)))
    full = jnp.where(same, full, 0.0) * REACT_STEP
    diagonal = (iota((rows, rows), 0) == iota((rows, rows), 1)).astype(jnp.float32)
    one = diagonal + full
    two = exact_dot(one, one)
    three = exact_dot(two, one)
    four = exact_dot(two, two)
    source = [
        exact_dot(spread * yields_ref[...], jnp.ones((tracers, wide), jnp.float32)) * REACT_STEP
    ]
    for power in (one, two, three):
        source.append(exact_dot(power, source[0]))
    head = jnp.concatenate([power[: 3 * Y] for power in (one, two, three)], axis=0)
    shape = (rows, wide)
    lane = iota(shape, 1)
    inject = jnp.zeros(shape, jnp.float32)
    for sub in range(SUB):
        hit = jnp.logical_and(lane // Y == sub, lane % Y == iota(shape, 0) % Y)
        inject = inject + jnp.where(hit, source[SUB - 1 - sub], 0.0)
    return head, four, inject[:, : SUB * Y], [v[: 3 * Y] for v in source[: SUB - 1]]


def stack(flat, wide):
    return jnp.concatenate(
        [flat[:, i * wide : (i + 1) * wide] for i in range(flat.shape[1] // wide)], axis=0
    )


def unstack(tall, Y):
    return jnp.concatenate(
        [tall[i * Y : (i + 1) * Y] for i in range(tall.shape[0] // Y)], axis=1
    )


def plan(span):
    return (3, (0, 2, 1)) if span % 3 == 0 else (1, (0,))


def kernel(
    regions, groups, sects,
    solute, heat_hbm, east_hbm, north_hbm, layers_hbm, rates_hbm, yields_hbm,
    tracers_out, heat_out,
    layers_in, rates_ref, yields_ref,
    state, ysend, yrecv, coef, final,
    in_send, in_recv, halo_send, halo_recv, out_send, out_recv, local_sem, load_sem,
):
    region, group, sect = (lax.axis_index(a) for a in ("region", "tracer", "sect"))
    own, wide, Y = solute.shape[0], solute.shape[2], layers_in.shape[0]
    tracers = own * groups
    block = heat_hbm.shape[0] // groups
    span = block // Y
    fields = tracers + 1
    every = fields + 3

    def place(reg, t):
        return t + (reg % 2) * (groups - 1 - 2 * t)

    part = place(region, group)
    last = groups - 1
    next_region = lax.rem(region + 1, regions)
    past_region = lax.rem(region + regions - 1, regions)
    east_region = jnp.where(part == last, next_region, region)
    west_region = jnp.where(part == 0, past_region, region)
    east_part = jnp.where(part == last, 0, part + 1)
    west_part = jnp.where(part == 0, last, part - 1)
    beside = {
        EAST: {"region": east_region, "tracer": place(east_region, east_part)},
        WEST: {"region": west_region, "tracer": place(west_region, west_part)},
        NORTH: {"sect": lax.rem(sect + 1, sects)},
        SOUTH: {"sect": lax.rem(sect + sects - 1, sects)},
    }
    peers = [lax.rem(group + d, groups) for d in range(1, groups)]

    def rows_of(t):
        return pl.ds(pl.multiple_of(place(region, t) * block, Y), block)

    mine = rows_of(group)
    slot = pl.ds(group * own, own)
    inner = pl.ds(Y, block)

    barrier = pltpu.get_barrier_semaphore()
    for peer in peers:
        pl.semaphore_signal(barrier, inc=1, device_id={"tracer": peer}, device_id_type=MESH)
    for side in range(4):
        pl.semaphore_signal(barrier, inc=1, device_id=beside[side], device_id_type=MESH)
    keep = pltpu.make_async_copy(
        solute.at[:, mine, :], state.at[0, slot, inner, :], local_sem.at[0, 0]
    )
    keep.start()
    loads = []
    for i, (source_ref, target_ref) in enumerate(
        (
            (layers_hbm, layers_in),
            (rates_hbm, rates_ref),
            (yields_hbm, yields_ref),
            (heat_hbm.at[mine, :], state.at[0, tracers, inner, :]),
            (east_hbm.at[mine, :], state.at[0, fields, inner, :]),
            (north_hbm.at[mine, :], state.at[0, fields + 1, inner, :]),
        )
    ):
        copy = pltpu.make_async_copy(source_ref, target_ref, load_sem.at[i])
        copy.start()
        loads.append(copy)
    pl.semaphore_wait(barrier, groups - 1 + 4)

    chunks, order = plan(span)
    deep = span // chunks
    piece = deep * Y

    def part_of(t, c):
        return pl.ds(pl.multiple_of(place(region, t) * block + c * piece, Y), piece)

    arriving = {}
    for i, c in enumerate(order):
        for d, peer in enumerate(peers):
            copy = pltpu.make_async_remote_copy(
                src_ref=solute.at[:, part_of(peer, c), :],
                dst_ref=state.at[0, slot, pl.ds(Y + c * piece, piece), :],
                send_sem=in_send.at[d, c],
                recv_sem=in_recv.at[d, c],
                device_id={"tracer": peer},
                device_id_type=MESH,
            )
            copy.start()
            arriving[c, d] = copy

    for copy in loads:
        copy.wait()
    total = layers_in.shape[1] * Y
    pick = (iota((total, layers_in.shape[1]), 0) // Y == iota((total, layers_in.shape[1]), 1))
    depth = lax.dot_general(
        pick.astype(jnp.bfloat16),
        layers_in[...].astype(jnp.float32).astype(jnp.bfloat16),
        (((1,), (1,)), ((), ())),
        preferred_element_type=jnp.float32,
    )
    depth = jnp.where(iota((total, Y), 0) % Y == iota((total, Y), 1), depth, 0.0)
    depth = half_dot(depth.astype(jnp.bfloat16), jnp.ones((Y, wide), jnp.bfloat16))
    coef[5] = (iota((total, wide), 1).astype(jnp.float32) < depth).astype(jnp.float32)
    state[0, fields + 2, inner, :] = coef[5, mine, :]

    head, four, inject, source = tables(rates_ref, yields_ref, tracers, wide, Y)
    head, four, inject = halves(head), halves(four), halves(inject)
    upper = (iota((wide, wide), 0) < iota((wide, wide), 1)).astype(jnp.bfloat16)
    level = iota((piece, wide), 1).astype(jnp.float32) + 0.5
    tile = (1, deep)
    source = [jnp.tile(v, tile) for v in source]

    def light(chl_abs):
        high, low = halves(chl_abs)
        above = half_dot(high, upper) + half_dot(low, upper)
        return jnp.exp(
            -(WATER_ATT / wide * level + CHL_ATT / wide * (above + 0.5 * chl_abs))
        )

    sent = []

    def exchange(step, c):
        count = every if step == 0 else fields
        some = pl.ds(0, count)
        moves = {}
        if c == chunks - 1:
            moves[EAST] = (
                state.at[step, some, pl.ds(block, Y), :],
                state.at[step, some, pl.ds(0, Y), :],
            )
        if c == 0:
            moves[WEST] = (
                state.at[step, some, pl.ds(Y, Y), :],
                state.at[step, some, pl.ds(block + Y, Y), :],
            )

        def send(moves):
            for side, (source_ref, target_ref) in moves.items():
                copy = pltpu.make_async_remote_copy(
                    src_ref=source_ref,
                    dst_ref=target_ref,
                    send_sem=halo_send.at[step, c, side],
                    recv_sem=halo_recv.at[step, c, side],
                    device_id=beside[side],
                    device_id_type=MESH,
                )
                copy.start()
                sent.append(copy)
                halos[step, c, side] = copy

        send(moves)
        for f in range(count):
            for side, y in ((0, 0), (1, Y - 1)):
                ysend[step, c, side, f] = state[
                    step, f, pl.ds(Y + c * piece + y, deep, stride=Y), :
                ]
        moves = {
            NORTH: (ysend.at[step, c, 1, some], yrecv.at[step, c, 1, some]),
            SOUTH: (ysend.at[step, c, 0, some], yrecv.at[step, c, 0, some]),
        }
        send(moves)

    halos = {}

    def beside_y(step, value, x, first, count):
        at = (count, Y, wide)
        row = iota(at, 1)
        some = pl.ds(first, count)
        above = jnp.broadcast_to(yrecv[step, x // deep, 0, some, pl.ds(x % deep, 1), :], at)
        below = jnp.broadcast_to(yrecv[step, x // deep, 1, some, pl.ds(x % deep, 1), :], at)
        up = jnp.where(row == Y - 1, above, pltpu.roll(value, Y - 1, 1))
        down = jnp.where(row == 0, below, pltpu.roll(value, 1, 1))
        return up, down

    keep.wait()
    for c in order:
        for d in range(len(peers)):
            arriving[c, d].wait_recv()
        exchange(0, c)

    leaving = []

    def leave(c):
        rows = pl.ds(c * piece, piece)
        out_rows = part_of(group, c)
        for d, peer in enumerate(peers):
            pairs = (
                (final.at[pl.ds(peer * own, own), rows, :], tracers_out.at[:, out_rows, :]),
                (final.at[tracers, rows, :], heat_out.at[out_rows, :]),
            )
            for i, (source_ref, target_ref) in enumerate(pairs):
                copy = pltpu.make_async_remote_copy(
                    src_ref=source_ref,
                    dst_ref=target_ref,
                    send_sem=out_send.at[d, c, i],
                    recv_sem=out_recv.at[d, c, i],
                    device_id={"tracer": peer},
                    device_id_type=MESH,
                )
                copy.start()
                leaving.append(copy)
        pairs = (
            (final.at[slot, rows, :], tracers_out.at[:, out_rows, :]),
            (final.at[tracers, rows, :], heat_out.at[out_rows, :]),
        )
        for i, (source_ref, target_ref) in enumerate(pairs):
            copy = pltpu.make_async_copy(source_ref, target_ref, local_sem.at[c, 1 + i])
            copy.start()
            leaving.append(copy)

    def advance(step, c):
        columns, heats, wets = [], [], []
        for x in range(c * deep, (c + 1) * deep):
            here = pl.ds((x + 1) * Y, Y)
            ahead = pl.ds((x + 2) * Y, Y)
            behind = pl.ds(x * Y, Y)
            cell = pl.ds(x * Y, Y)
            if step == 0:
                speed_wet = state[0, pl.ds(fields + 1, 2), here, :]
                up, down = beside_y(0, speed_wet, x, fields + 1, 2)
                wet = speed_wet[1]
                east = state[0, fields, here, :] * wet * state[0, fields + 2, ahead, :]
                west = state[0, fields, behind, :] * state[0, fields + 2, behind, :] * wet
                north = speed_wet[0] * wet * up[1]
                south = down[0] * down[1] * wet
                scaled = TIME_STEP * wet
                coef[0, cell, :] = wet - scaled * (
                    jnp.maximum(east, 0.0) - jnp.minimum(west, 0.0)
                    + jnp.maximum(north, 0.0) - jnp.minimum(south, 0.0)
                )
                coef[1, cell, :] = -scaled * jnp.minimum(east, 0.0)
                coef[2, cell, :] = scaled * jnp.maximum(west, 0.0)
                coef[3, cell, :] = -scaled * jnp.minimum(north, 0.0)
                coef[4, cell, :] = scaled * jnp.maximum(south, 0.0)
            value = state[step, pl.ds(0, fields), here, :]
            up, down = beside_y(step, value, x, 0, fields)
            moved = (
                coef[0, cell, :] * value
                + coef[1, cell, :] * state[step, pl.ds(0, fields), ahead, :]
                + coef[2, cell, :] * state[step, pl.ds(0, fields), behind, :]
                + coef[3, cell, :] * up
                + coef[4, cell, :] * down
            )
            columns.append(moved[:tracers].reshape(tracers * Y, wide))
            heats.append(moved[tracers])
            wets.append(state[0, fields + 2, here, :])
        mixed = jnp.concatenate(columns, axis=1)
        parts = halves(mixed)
        ahead_rows = dot3(head, parts)
        result = dot3(four, parts)
        rates = []
        for sub in range(SUB):
            if sub == 0:
                rows = mixed[: 3 * Y]
            else:
                rows = ahead_rows[(sub - 1) * 3 * Y : sub * 3 * Y]
                for i, rate in enumerate(rates):
                    rows = rows + source[sub - 1 - i] * jnp.concatenate([rate] * 3, axis=0)
            nutrient, chl, phyto = rows[:Y], rows[Y : 2 * Y], rows[2 * Y :]
            shade = unstack(light(jnp.abs(stack(chl, wide))), Y)
            rates.append(
                GROWTH_MAX * shade * nutrient / (jnp.abs(nutrient) + HALF_SAT) * phyto
            )
        result = result + dot3(inject, halves(jnp.concatenate(rates, axis=0)))
        chl_abs = jnp.abs(stack(result[Y : 2 * Y], wide))
        heating = HEAT_GAIN * chl_abs * light(chl_abs)
        heat = jnp.concatenate(heats, axis=0) + TIME_STEP * jnp.concatenate(wets, axis=0) * heating
        if step < STEPS - 1:
            target, base = state.at[step + 1], Y + c * piece
        else:
            target, base = final, c * piece
        for x in range(deep):
            target[pl.ds(0, tracers), pl.ds(base + x * Y, Y), :] = result[
                :, x * wide : (x + 1) * wide
            ].reshape(tracers, Y, wide)
        target[tracers, pl.ds(base, piece), :] = heat

    for step in range(STEPS):
        for c in order:
            for side in (NORTH, SOUTH):
                halos[step, c, side].wait_recv()
            if c == 0:
                halos[step, chunks - 1, EAST].wait_recv()
            if c == chunks - 1:
                halos[step, 0, WEST].wait_recv()
            advance(step, c)
            if step < STEPS - 1:
                exchange(step + 1, c)
            else:
                leave(c)
    for copy in leaving:
        copy.wait()
    for copy in sent + list(arriving.values()):
        copy.wait_send()

SHARE = 5
FIRST = 3


def wide_halves(x):
    high, low = halves(x)
    return jnp.concatenate([high, high, low], axis=1)


def tall_halves(x):
    high, low = halves(x)
    return jnp.concatenate([high, low, high], axis=0)


def pair_tables(rates_ref, yields_ref, tracers, wide, Y):
    rows = tracers * Y
    spread = (iota((rows, tracers), 0) // Y == iota((rows, tracers), 1)).astype(jnp.float32)
    same = iota((rows, rows), 0) % Y == iota((rows, rows), 1) % Y
    full = exact_dot(exact_dot(spread, rates_ref[...]), spread, ((1,), (1,)))
    full = jnp.where(same, full, 0.0) * REACT_STEP
    diagonal = (iota((rows, rows), 0) == iota((rows, rows), 1)).astype(jnp.float32)
    one = diagonal + full
    two = exact_dot(one, one)
    three = exact_dot(two, one)
    four = exact_dot(two, two)
    source = [
        exact_dot(spread * yields_ref[...], jnp.ones((tracers, wide), jnp.float32)) * REACT_STEP
    ]
    for power in (one, two, three):
        source.append(exact_dot(power, source[0]))
    powers = jnp.concatenate([power[: 3 * Y] for power in (one, two, three)] + [four], axis=0)
    shape = (rows, wide)
    lane = iota(shape, 1)
    inject = jnp.zeros(shape, jnp.float32)
    for sub in range(SUB):
        hit = jnp.logical_and(lane // Y == sub, lane % Y == iota(shape, 0) % Y)
        inject = inject + jnp.where(hit, source[SUB - 1 - sub], 0.0)
    return (
        wide_halves(powers),
        wide_halves(inject[:, : SUB * Y]),
        [v[: 3 * Y] for v in source],
    )


def pair_plan(half):
    low = -SHARE - STEPS
    ranges = [(half - STEPS, STEPS)]
    for at, end in ((SHARE - STEPS, half - STEPS), (low, SHARE - STEPS)):
        while at < end:
            size = min(STEPS, end - at)
            ranges.append((at, size))
            at += size
    return low, ranges


def pair_kernel(
    regions, sects,
    solute, heat_hbm, east_hbm, north_hbm, layers_hbm, rates_hbm, yields_hbm,
    tracers_out, heat_out,
    layers_in, rates_ref, yields_ref, state, coef, wets, final, measure,
    send_sem, recv_sem,
):
    groups = 2
    region, group, sect = (lax.axis_index(a) for a in ("region", "tracer", "sect"))
    own, X, Y, wide = solute.shape
    half = X // groups
    tracers = own * groups
    fields = tracers + 1
    base = STEPS + 1
    low, ranges = pair_plan(half)
    reach = half - low
    odd = region % 2
    part = group + odd * (1 - 2 * group)
    peer = 1 - group

    def pick(flag, a, b):
        return a + flag * (b - a)

    def P(u, k, flag=part):
        return pick(flag, half + STEPS - u - k, u - low)

    def B(u, k, flag=part):
        return pick(flag, half - u - k, half + u)

    outer_region = lax.rem(region + pick(part, regions - 1, 1), regions)
    outer_part = 1 - part
    outer_odd = outer_region % 2
    beside = {"region": outer_region, "tracer": outer_part + outer_odd * (1 - 2 * outer_part)}
    north = {"sect": lax.rem(sect + 1, sects)}
    south = {"sect": lax.rem(sect + sects - 1, sects)}
    across = {"tracer": peer}
    mine, other = pl.ds(group * own, own), pl.ds(peer * own, own)

    names, lines = {}, {}

    def slot(name):
        return names.setdefault(name, len(names))

    def tally(name, ref):
        lines[name] = lines.get(name, 0) + math.prod(ref.shape) // wide

    def settle(name, sems=recv_sem):
        some = measure.at[pl.ds(0, lines[name])]
        at = slot(name) if sems is recv_sem else int(name[4:])
        with jax.named_scope(name):
            pltpu.make_async_copy(some, some, sems.at[at]).wait()

    def local(name, source_ref, target_ref):
        tally(name, target_ref)
        pltpu.make_async_copy(source_ref, target_ref, recv_sem.at[slot(name)]).start()

    def remote(name, source_ref, target_ref, device, turn=0):
        tally(name, target_ref)
        tally(f"sent{turn}", source_ref)
        push(name, source_ref, target_ref, device, turn)

    def push(name, source_ref, target_ref, device, turn=0):
        pltpu.make_async_remote_copy(
            src_ref=source_ref,
            dst_ref=target_ref,
            send_sem=send_sem.at[turn],
            recv_sem=recv_sem.at[slot(name)],
            device_id=device,
            device_id_type=MESH,
        ).start()

    raw = state.at[0]
    body = pl.ds(base, Y)
    blank = jnp.zeros((tracers + 4, 1, STEPS, wide), jnp.float32)
    for u in (low, half, half + 1, half + 2):
        for row in (base - STEPS, base + Y):
            raw[:, pl.ds(P(u, 1), 1), pl.ds(row, STEPS), :] = blank
    barrier = pltpu.get_barrier_semaphore()
    for device in (across, beside, north, south):
        pl.semaphore_signal(barrier, inc=1, device_id=device, device_id_type=MESH)

    small = [
        pltpu.make_async_copy(source_ref, target_ref, recv_sem.at[slot(f"small{i}")])
        for i, (source_ref, target_ref) in enumerate(
            ((layers_hbm, layers_in), (rates_hbm, rates_ref), (yields_hbm, yields_ref))
        )
    ]
    for copy in small:
        copy.start()
    p_all, b_all = P(low, reach), B(low, reach)
    in_block = pl.ds(b_all, reach)
    in_state = pl.ds(p_all, reach)
    extra = ((heat_hbm, tracers), (east_hbm, fields), (north_hbm, fields + 1))
    local("loads", solute.at[:, in_block], raw.at[mine, in_state, body])
    for ref, field in extra:
        local("loads", ref.at[in_block], raw.at[field, in_state, body])

    with jax.named_scope("barrier"):
        pl.semaphore_wait(barrier, 4)

    def cross(i):
        u, k = ranges[i]
        remote(
            f"x{i}",
            solute.at[:, pl.ds(B(u, k, 1 - part), k)],
            raw.at[mine, pl.ds(P(u, k, 1 - part), k), body],
            across,
        )

    edge = half - STEPS
    edge_block = pl.ds(B(edge, STEPS), STEPS)
    edge_state = pl.ds(P(edge, STEPS), STEPS)
    past = pl.ds(pick(part, reach, 0), STEPS)
    cross(0)
    remote("outer", solute.at[:, edge_block], raw.at[mine, past, body], beside)
    for ref, field in extra:
        remote("outer", ref.at[edge_block], raw.at[field, past, body], beside)
    for i in range(1, len(ranges)):
        cross(i)
    far = sect % 2

    def both_sides(send):
        for first in (0, 1):
            @pl.when(far == first)
            def _():
                for side in (first, 1 - first):
                    send(side, (south, north)[side])

    def halo_row(side, deep=STEPS):
        return pl.ds(base - deep if side else base + Y, deep)

    def tally_sides(name, refs):
        for ref in refs:
            for _ in range(2):
                tally(name, ref)
                tally("sent0", ref)

    def direct_rows(name, u, k):
        b, p = pl.ds(B(u, k), k), pl.ds(P(u, k), k)
        refs = [(solute.at[:, b], mine)] + [(ref.at[b], field) for ref, field in extra]

        def send(side, device):
            block_rows = pl.ds(Y - STEPS if side else 0, STEPS)
            for ref, field in refs:
                rows = ref.at[:, :, block_rows] if ref is refs[0][0] else ref.at[:, block_rows]
                push(name, rows, raw.at[field, p, halo_row(side)], device)

        both_sides(send)
        tally_sides(name, [raw.at[field, p, halo_row(0)] for _, field in refs])

    def beside_rows(name, some, u, k, deep=STEPS):
        place = pl.ds(P(u, k), k)

        def send(side, device):
            start = base + Y - deep if side else base
            push(
                name,
                raw.at[some, place, pl.ds(start, deep)],
                raw.at[some, place, halo_row(side, deep)],
                device,
            )

        both_sides(send)
        tally_sides(name, [raw.at[some, place, halo_row(0, deep)]])

    near = 1 + -(-(FIRST + 2 * STEPS) // STEPS)
    cone = min((near - 1) * STEPS, edge + STEPS + STEPS - SHARE)
    cone_at = max(low + 1, SHARE - STEPS)
    cone_end = SHARE - STEPS + cone
    direct_rows("rows", cone_at, cone_end - cone_at)
    if cone_end < half:
        direct_rows("rest", cone_end, half - cone_end)
    if low + 1 < cone_at:
        direct_rows("rest", low + 1, cone_at - low - 1)

    for copy in small:
        copy.wait()
    total = X * Y
    pick_rows = iota((total, X), 0) // Y == iota((total, X), 1)
    depth = lax.dot_general(
        pick_rows.astype(jnp.bfloat16),
        layers_in[...].astype(jnp.float32).astype(jnp.bfloat16),
        (((1,), (1,)), ((), ())),
        preferred_element_type=jnp.float32,
    )
    depth = jnp.where(iota((total, Y), 0) % Y == iota((total, Y), 1), depth, 0.0)
    depth = half_dot(depth.astype(jnp.bfloat16), jnp.ones((Y, wide), jnp.bfloat16))
    wets[...] = (iota((total, wide), 1).astype(jnp.float32) < depth).astype(jnp.float32).reshape(
        X, Y, wide
    )
    wet_field = fields + 2
    raw[wet_field, in_state, body, :] = wets[in_block]
    remote("outer", raw.at[wet_field, edge_state, body], raw.at[wet_field, past, body], beside)
    beside_rows("rows", pl.ds(wet_field, 1), low + 1, reach - 1)

    with jax.named_scope("make_tables"):
        powers, inject, source = pair_tables(rates_ref, yields_ref, tracers, wide, Y)
    shape = (wide, wide)
    upper = (iota(shape, 0) < iota(shape, 1)).astype(jnp.float32)
    upper = upper + 0.5 * (iota(shape, 0) == iota(shape, 1)).astype(jnp.float32)
    upper = jnp.concatenate([upper.astype(jnp.bfloat16)] * 2, axis=0)
    level = (iota((Y, wide), 1).astype(jnp.float32) + 0.5) * (-WATER_ATT / wide)
    settle("loads")

    def light(chl_abs):
        high, low_part = halves(chl_abs)
        above = half_dot(jnp.concatenate([high, low_part], axis=1), upper)
        tall = jnp.concatenate([level] * (chl_abs.shape[0] // Y), axis=0)
        return jnp.exp(tall - CHL_ATT / wide * above)

    done = set()

    def once(name):
        fresh = name not in done
        done.add(name)
        return fresh

    def arrive(i):
        if once(f"x{i}"):
            settle(f"x{i}")
            u, k = ranges[i]
            some = pl.ds(P(u, k), k)
            if i == 0:
                remote("outer", raw.at[other, some, body], raw.at[other, past, body], beside)
            skip = int(u == low)
            beside_rows(f"y{i}", other, u + skip, k - skip)

    def arrive_outer():
        arrive(0)
        if once("outer"):
            settle("outer")
            beside_rows("corner", slice(None), half, STEPS - 1, STEPS - 1)

    def ready(first, last):
        if once("rows"):
            settle("rows")
        if (first < cone_at - 1 or last >= cone_end) and "rest" in lines and once("rest"):
            settle("rest")
        for i, (u, k) in enumerate(ranges):
            if u <= last and first < u + k:
                arrive(i)
                if once(f"y{i}"):
                    settle(f"y{i}")
        if last >= half:
            arrive_outer()
            if once("corner"):
                settle("corner")

    windows = [
        (base - STEPS + 1, base + Y + STEPS - 1 - Y),
        (base - 1, base + 1),
        (base,),
    ]

    def stencil(step, p, r):
        here = pl.ds(r, Y)
        up_rows, down_rows = pl.ds(r + 1, Y), pl.ds(r - 1, Y)
        if step == 0:
            wet = raw[wet_field, p, here, :]
            south_wet = raw[wet_field, p, down_rows, :]
            east = raw[fields, p, here, :] * wet * raw[wet_field, p + 1, here, :]
            west = raw[fields, p - 1, here, :] * raw[wet_field, p - 1, here, :] * wet
            up = raw[fields + 1, p, here, :] * wet * raw[wet_field, p, up_rows, :]
            down = raw[fields + 1, p, down_rows, :] * south_wet * wet
            scaled = TIME_STEP * wet
            c = [
                wet
                - scaled
                * (
                    jnp.maximum(east, 0.0) - jnp.minimum(west, 0.0)
                    + jnp.maximum(up, 0.0) - jnp.minimum(down, 0.0)
                ),
                -scaled * jnp.minimum(east, 0.0),
                scaled * jnp.maximum(west, 0.0),
                -scaled * jnp.minimum(up, 0.0),
                scaled * jnp.maximum(down, 0.0),
                scaled,
            ]
            for i, v in enumerate(c):
                coef[i, p, here, :] = v
        else:
            c = [coef[i, p, here, :] for i in range(6)]
        some = pl.ds(0, fields)
        moved = (
            c[0] * state[step, some, p, here, :]
            + c[1] * state[step, some, p + 1, here, :]
            + c[2] * state[step, some, p - 1, here, :]
            + c[3] * state[step, some, p, up_rows, :]
            + c[4] * state[step, some, p, down_rows, :]
        )
        return moved, c[5]

    def advance(*work):
        work = [item for item in work if item[2] > 0]
        for step, u, k in work:
            if step == 0:
                ready(u - 1, u + k)
        with jax.named_scope("go" + "_".join(f"{s}:{u}:{k}" for s, u, k in work)):
            compute(work)

    def compute(work):
        tiles = []
        for step, u, k in work:
            p = P(u, k)
            for i in range(k):
                for r in windows[step]:
                    tiles.append((step, p + i, r))
        columns, heats, scales = [], [], []
        for step, p, r in tiles:
            moved, scaled = stencil(step, p, r)
            columns.append(moved[:tracers].reshape(tracers * Y, wide))
            heats.append(moved[tracers])
            scales.append(scaled)
        n = len(tiles)
        mixed = jnp.concatenate(columns, axis=1)
        ahead = half_dot(powers, tall_halves(mixed))
        block = 3 * Y
        result = ahead[3 * block :]

        def part_of(rows, i):
            return stack(rows[i * Y : (i + 1) * Y], wide)

        def spread(v, i):
            return jnp.concatenate([v[i * Y : (i + 1) * Y]] * n, axis=0)

        rates = []
        for sub in range(SUB):
            rows = mixed[:block] if sub == 0 else ahead[(sub - 1) * block : sub * block]
            value = []
            for i in range(3):
                v = part_of(rows, i)
                for j, rate in enumerate(rates):
                    v = v + spread(source[sub - 1 - j], i) * rate
                value.append(v)
            nutrient, chl, phyto = value
            rates.append(
                light(jnp.abs(chl)) * (nutrient / (jnp.abs(nutrient) + HALF_SAT) * phyto)
            )
        chl = part_of(result, 1)
        for j, rate in enumerate(rates):
            chl = chl + spread(source[SUB - 1 - j], 1) * rate
        chl_abs = jnp.abs(chl)
        flat = jnp.concatenate([unstack(rate, Y) for rate in rates], axis=0)
        result = result + half_dot(inject, tall_halves(flat))
        heat = jnp.concatenate(heats, axis=0) + HEAT_GAIN * (
            jnp.concatenate(scales, axis=0) * chl_abs * light(chl_abs)
        )
        for i, (step, p, r) in enumerate(tiles):
            value = result[:, i * wide : (i + 1) * wide].reshape(tracers, Y, wide)
            if step < STEPS - 1:
                here = pl.ds(r, Y)
                state[step + 1, pl.ds(0, tracers), p, here, :] = value
                state[step + 1, tracers, p, here, :] = heat[i * Y : (i + 1) * Y]
            else:
                final[pl.ds(0, tracers), p, :, :] = value
                final[tracers, p, :, :] = heat[i * Y : (i + 1) * Y]

    def leave(u, k):
        if k <= 0:
            return
        some, place = pl.ds(P(u, k), k), pl.ds(B(u, k), k)
        if u >= SHARE:
            remote("arrivals", final.at[other, some], tracers_out.at[:, place], across, 1)
            remote("arrivals", final.at[tracers, some], heat_out.at[place], across, 1)
        local("leaving", final.at[mine, some], tracers_out.at[:, place])
        local("leaving", final.at[tracers, some], heat_out.at[place])

    for action in schedule(half):
        if action[0] == "x":
            arrive(action[1])
        elif action[0] == "z":
            arrive_outer()
        elif action[0] == "go":
            advance(*action[1:])
        else:
            leave(*action[1:])
    settle("leaving")
    settle("arrivals")
    settle("sent0", send_sem)
    settle("sent1", send_sem)


def schedule(half):
    count = len(pair_plan(half)[1])
    h, a, b = SHARE, FIRST, half - STEPS
    near = 1 + -(-(a + 2 * STEPS) // STEPS)
    inner = [[(s, -h - 2 + s, 2 * h)] if h else [] for s in range(STEPS)]
    own = 1 + -(-(b - h + STEPS) // STEPS)
    rest = b - h - a
    late = [("x", i) for i in range(own, count)]
    plan = [("x", i) for i in range(own)]
    plan += [("go", (0, h - 2, a + 4)), ("z",), *late[:1], ("go", (1, h - 1, a + 2)), *late[1:2]]
    plan += [("go", (2, h, a), (0, h + a + 2, rest)), ("out", h, a)]
    plan += [("go", (1, h + a + 1, rest), (0, b + 2, 3)), *late[2:]]
    plan += [("go", (2, h + a, rest), (1, b + 1, 3)), ("out", h + a, rest)]
    plan += [("go", (2, b, 3)), ("out", b, 3)]
    for s in range(STEPS if h else 0):
        plan.append(("go", *inner[s]))
    return plan + ([("out", -h, 2 * h)] if h else [])


def paired(shape, groups, regions, sects):
    return (
        groups == 2 and regions > 1 and regions % 2 == 0 and sects > 1
        and shape[2] == 8 and shape[3] == 128 and shape[1] % 2 == 0 and shape[1] >= 24
        and shape[0] * groups * shape[2] == 128
    )


def write_out(mixture, heat, mixture_out, heat_out, sems):
    own = mixture.shape[0]
    copies = [
        pltpu.make_async_copy(mixture.at[i], mixture_out.at[i], sems.at[i]) for i in range(own)
    ]
    copies.append(pltpu.make_async_copy(heat, heat_out, sems.at[own]))
    for copy in copies:
        copy.start()
    for copy in copies:
        copy.wait()


def pair_call(solute, thermal, eastward, northward, layers, rates, yields, regions, sects):
    own, X, Y, wide = solute.shape
    tracers = own * 2
    half = X // 2
    low, ranges = pair_plan(half)
    columns = half - low + STEPS
    operands = [
        pltpu.with_memory_space_constraint(v, pltpu.HBM)
        for v in (solute, thermal, eastward, northward, layers.T, rates, yields.reshape(1, tracers))
    ]
    hbm = pl.BlockSpec(memory_space=pltpu.HBM)
    free = pl.BlockSpec(memory_space=pl.ANY)
    dma = pltpu.SemaphoreType.DMA
    mixture, heat = pl.pallas_call(
        functools.partial(pair_kernel, regions, sects),
        out_shape=(
            jax.ShapeDtypeStruct(solute.shape, jnp.float32),
            jax.ShapeDtypeStruct(thermal.shape, jnp.float32),
        ),
        in_specs=[hbm] * 7,
        out_specs=(free, free),
        scratch_shapes=[
            pltpu.VMEM((Y, X), jnp.int32),
            pltpu.VMEM((tracers, tracers), jnp.float32),
            pltpu.VMEM((1, tracers), jnp.float32),
            pltpu.VMEM((STEPS, tracers + 4, columns, 2 * Y, wide), jnp.float32),
            pltpu.VMEM((6, columns, 2 * Y, wide), jnp.float32),
            pltpu.VMEM((X, Y, wide), jnp.float32),
            pltpu.VMEM((tracers + 1, columns, Y, wide), jnp.float32),
            pltpu.VMEM((MEASURE, wide), jnp.float32),
            dma((2,)),
            dma((len(ranges) * 2 + 10,)),
        ],
        compiler_params=pltpu.CompilerParams(
            collective_id=0, has_side_effects=True, vmem_limit_bytes=40 << 20
        ),
    )(*operands)
    return pl.pallas_call(
        write_out,
        out_shape=(
            jax.ShapeDtypeStruct(solute.shape, jnp.float32),
            jax.ShapeDtypeStruct(thermal.shape, jnp.float32),
        ),
        in_specs=[free] * 2,
        out_specs=(hbm, hbm),
        scratch_shapes=[dma((own + 1,))],
        compiler_params=pltpu.CompilerParams(vmem_limit_bytes=1 << 20),
    )(mixture, heat)


MEASURE = 8192


def solution(mesh):
    regions, groups, sects = (mesh.shape[a] for a in ("region", "tracer", "sect"))

    def body(solute, thermal, eastward, northward, layers, rates, yields):
        if paired(solute.shape, groups, regions, sects):
            return pair_call(
                solute, thermal, eastward, northward, layers, rates, yields, regions, sects
            )
        own, rows, cols, wide = solute.shape
        tracers = own * groups
        span = rows // groups
        fields = tracers + 1
        flat = (rows * cols, wide)
        free, hbm = pl.BlockSpec(memory_space=pl.ANY), pl.BlockSpec(memory_space=pltpu.HBM)
        dma = pltpu.SemaphoreType.DMA
        peers = max(groups - 1, 1)
        chunks = plan(span)[0]
        mixture, heat = pl.pallas_call(
            functools.partial(kernel, regions, groups, sects),
            out_shape=(
                jax.ShapeDtypeStruct((own, *flat), jnp.float32),
                jax.ShapeDtypeStruct(flat, jnp.float32),
            ),
            in_specs=[hbm] * 7,
            out_specs=(free, free),
            scratch_shapes=[
                pltpu.VMEM((cols, rows), jnp.int32),
                pltpu.VMEM((tracers, tracers), jnp.float32),
                pltpu.VMEM((1, tracers), jnp.float32),
                pltpu.VMEM((STEPS, fields + 3, (span + 2) * cols, wide), jnp.float32),
                pltpu.VMEM((STEPS, chunks, 2, fields + 3, span // chunks, wide), jnp.float32),
                pltpu.VMEM((STEPS, chunks, 2, fields + 3, span // chunks, wide), jnp.float32),
                pltpu.VMEM((6, *flat), jnp.float32),
                pltpu.VMEM((fields, span * cols, wide), jnp.float32),
                dma((peers, chunks)),
                dma((peers, chunks)),
                dma((STEPS, chunks, 4)),
                dma((STEPS, chunks, 4)),
                dma((peers, chunks, 2)),
                dma((peers, chunks, 2)),
                dma((chunks, 3)),
                dma((6,)),
            ],
            compiler_params=pltpu.CompilerParams(
                collective_id=0, has_side_effects=True, vmem_limit_bytes=60 << 20
            ),
        )(
            solute.reshape(own, *flat),
            thermal.reshape(flat),
            eastward.reshape(flat),
            northward.reshape(flat),
            layers.T,
            rates,
            yields.reshape(1, tracers),
        )
        return mixture.reshape(solute.shape), heat.reshape(thermal.shape)

    return jax.shard_map(
        body,
        mesh=mesh,
        in_specs=(
            P("tracer", "region", "sect", None),
            P("region", "sect", None),
            P("region", "sect", None),
            P("region", "sect", None),
            P("region", "sect"),
            P(),
            P(),
        ),
        out_specs=(P("tracer", "region", "sect", None), P("region", "sect", None)),
        check_vma=False,
    )
```

```python
import functools
import math

import jax
import jax.numpy as jnp
from jax import lax
from jax.experimental import pallas as pl
from jax.experimental.pallas import tpu as pltpu
from jax.sharding import PartitionSpec as P

STEPS = 3
SUB = 4

TIME_STEP = 0.2
REACT_STEP = 0.1
GROWTH_MAX = 1.0
HALF_SAT = 0.5
WATER_ATT = 3.0
CHL_ATT = 2.0
HEAT_GAIN = 0.5

MESH = pl.DeviceIdType.MESH
HIGHEST = lax.Precision.HIGHEST
EAST, WEST, NORTH, SOUTH = range(4)


def iota(shape, dim):
    return lax.broadcasted_iota(jnp.int32, shape, dim)


def exact_dot(a, b, dims=((1,), (0,))):
    return lax.dot_general(
        a, b, (dims, ((), ())), precision=HIGHEST, preferred_element_type=jnp.float32
    )


def halves(x):
    high = x.astype(jnp.bfloat16)
    return high, (x - high.astype(jnp.float32)).astype(jnp.bfloat16)


def half_dot(a, b):
    return jnp.dot(a, b, preferred_element_type=jnp.float32)


def dot3(a, b):
    return half_dot(a[0], b[0]) + half_dot(a[1], b[0]) + half_dot(a[0], b[1])


def tables(rates_ref, yields_ref, tracers, wide, Y):
    rows = tracers * Y
    spread = (iota((rows, tracers), 0) // Y == iota((rows, tracers), 1)).astype(jnp.float32)
    same = iota((rows, rows), 0) % Y == iota((rows, rows), 1) % Y
    full = exact_dot(exact_dot(spread, rates_ref[...]), spread, ((1,), (1,)))
    full = jnp.where(same, full, 0.0) * REACT_STEP
    diagonal = (iota((rows, rows), 0) == iota((rows, rows), 1)).astype(jnp.float32)
    one = diagonal + full
    two = exact_dot(one, one)
    three = exact_dot(two, one)
    four = exact_dot(two, two)
    source = [
        exact_dot(spread * yields_ref[...], jnp.ones((tracers, wide), jnp.float32)) * REACT_STEP
    ]
    for power in (one, two, three):
        source.append(exact_dot(power, source[0]))
    head = jnp.concatenate([power[: 3 * Y] for power in (one, two, three)], axis=0)
    shape = (rows, wide)
    lane = iota(shape, 1)
    inject = jnp.zeros(shape, jnp.float32)
    for sub in range(SUB):
        hit = jnp.logical_and(lane // Y == sub, lane % Y == iota(shape, 0) % Y)
        inject = inject + jnp.where(hit, source[SUB - 1 - sub], 0.0)
    return head, four, inject[:, : SUB * Y], [v[: 3 * Y] for v in source[: SUB - 1]]


def stack(flat, wide):
    return jnp.concatenate(
        [flat[:, i * wide : (i + 1) * wide] for i in range(flat.shape[1] // wide)], axis=0
    )


def unstack(tall, Y):
    return jnp.concatenate(
        [tall[i * Y : (i + 1) * Y] for i in range(tall.shape[0] // Y)], axis=1
    )


def plan(span):
    return (3, (0, 2, 1)) if span % 3 == 0 else (1, (0,))


def kernel(
    regions, groups, sects,
    solute, heat_hbm, east_hbm, north_hbm, layers_hbm, rates_hbm, yields_hbm,
    tracers_out, heat_out,
    layers_in, rates_ref, yields_ref,
    state, ysend, yrecv, coef, final,
    in_send, in_recv, halo_send, halo_recv, out_send, out_recv, local_sem, load_sem,
):
    region, group, sect = (lax.axis_index(a) for a in ("region", "tracer", "sect"))
    own, wide, Y = solute.shape[0], solute.shape[2], layers_in.shape[0]
    tracers = own * groups
    block = heat_hbm.shape[0] // groups
    span = block // Y
    fields = tracers + 1
    every = fields + 3

    def place(reg, t):
        return t + (reg % 2) * (groups - 1 - 2 * t)

    part = place(region, group)
    last = groups - 1
    next_region = lax.rem(region + 1, regions)
    past_region = lax.rem(region + regions - 1, regions)
    east_region = jnp.where(part == last, next_region, region)
    west_region = jnp.where(part == 0, past_region, region)
    east_part = jnp.where(part == last, 0, part + 1)
    west_part = jnp.where(part == 0, last, part - 1)
    beside = {
        EAST: {"region": east_region, "tracer": place(east_region, east_part)},
        WEST: {"region": west_region, "tracer": place(west_region, west_part)},
        NORTH: {"sect": lax.rem(sect + 1, sects)},
        SOUTH: {"sect": lax.rem(sect + sects - 1, sects)},
    }
    peers = [lax.rem(group + d, groups) for d in range(1, groups)]

    def rows_of(t):
        return pl.ds(pl.multiple_of(place(region, t) * block, Y), block)

    mine = rows_of(group)
    slot = pl.ds(group * own, own)
    inner = pl.ds(Y, block)

    barrier = pltpu.get_barrier_semaphore()
    for peer in peers:
        pl.semaphore_signal(barrier, inc=1, device_id={"tracer": peer}, device_id_type=MESH)
    for side in range(4):
        pl.semaphore_signal(barrier, inc=1, device_id=beside[side], device_id_type=MESH)
    keep = pltpu.make_async_copy(
        solute.at[:, mine, :], state.at[0, slot, inner, :], local_sem.at[0, 0]
    )
    keep.start()
    loads = []
    for i, (source_ref, target_ref) in enumerate(
        (
            (layers_hbm, layers_in),
            (rates_hbm, rates_ref),
            (yields_hbm, yields_ref),
            (heat_hbm.at[mine, :], state.at[0, tracers, inner, :]),
            (east_hbm.at[mine, :], state.at[0, fields, inner, :]),
            (north_hbm.at[mine, :], state.at[0, fields + 1, inner, :]),
        )
    ):
        copy = pltpu.make_async_copy(source_ref, target_ref, load_sem.at[i])
        copy.start()
        loads.append(copy)
    pl.semaphore_wait(barrier, groups - 1 + 4)

    chunks, order = plan(span)
    deep = span // chunks
    piece = deep * Y

    def part_of(t, c):
        return pl.ds(pl.multiple_of(place(region, t) * block + c * piece, Y), piece)

    arriving = {}
    for i, c in enumerate(order):
        for d, peer in enumerate(peers):
            copy = pltpu.make_async_remote_copy(
                src_ref=solute.at[:, part_of(peer, c), :],
                dst_ref=state.at[0, slot, pl.ds(Y + c * piece, piece), :],
                send_sem=in_send.at[d, c],
                recv_sem=in_recv.at[d, c],
                device_id={"tracer": peer},
                device_id_type=MESH,
            )
            copy.start()
            arriving[c, d] = copy

    for copy in loads:
        copy.wait()
    total = layers_in.shape[1] * Y
    pick = (iota((total, layers_in.shape[1]), 0) // Y == iota((total, layers_in.shape[1]), 1))
    depth = lax.dot_general(
        pick.astype(jnp.bfloat16),
        layers_in[...].astype(jnp.float32).astype(jnp.bfloat16),
        (((1,), (1,)), ((), ())),
        preferred_element_type=jnp.float32,
    )
    depth = jnp.where(iota((total, Y), 0) % Y == iota((total, Y), 1), depth, 0.0)
    depth = half_dot(depth.astype(jnp.bfloat16), jnp.ones((Y, wide), jnp.bfloat16))
    coef[5] = (iota((total, wide), 1).astype(jnp.float32) < depth).astype(jnp.float32)
    state[0, fields + 2, inner, :] = coef[5, mine, :]

    head, four, inject, source = tables(rates_ref, yields_ref, tracers, wide, Y)
    head, four, inject = halves(head), halves(four), halves(inject)
    upper = (iota((wide, wide), 0) < iota((wide, wide), 1)).astype(jnp.bfloat16)
    level = iota((piece, wide), 1).astype(jnp.float32) + 0.5
    tile = (1, deep)
    source = [jnp.tile(v, tile) for v in source]

    def light(chl_abs):
        high, low = halves(chl_abs)
        above = half_dot(high, upper) + half_dot(low, upper)
        return jnp.exp(
            -(WATER_ATT / wide * level + CHL_ATT / wide * (above + 0.5 * chl_abs))
        )

    sent = []

    def exchange(step, c):
        count = every if step == 0 else fields
        some = pl.ds(0, count)
        moves = {}
        if c == chunks - 1:
            moves[EAST] = (
                state.at[step, some, pl.ds(block, Y), :],
                state.at[step, some, pl.ds(0, Y), :],
            )
        if c == 0:
            moves[WEST] = (
                state.at[step, some, pl.ds(Y, Y), :],
                state.at[step, some, pl.ds(block + Y, Y), :],
            )

        def send(moves):
            for side, (source_ref, target_ref) in moves.items():
                copy = pltpu.make_async_remote_copy(
                    src_ref=source_ref,
                    dst_ref=target_ref,
                    send_sem=halo_send.at[step, c, side],
                    recv_sem=halo_recv.at[step, c, side],
                    device_id=beside[side],
                    device_id_type=MESH,
                )
                copy.start()
                sent.append(copy)
                halos[step, c, side] = copy

        send(moves)
        for f in range(count):
            for side, y in ((0, 0), (1, Y - 1)):
                ysend[step, c, side, f] = state[
                    step, f, pl.ds(Y + c * piece + y, deep, stride=Y), :
                ]
        moves = {
            NORTH: (ysend.at[step, c, 1, some], yrecv.at[step, c, 1, some]),
            SOUTH: (ysend.at[step, c, 0, some], yrecv.at[step, c, 0, some]),
        }
        send(moves)

    halos = {}

    def beside_y(step, value, x, first, count):
        at = (count, Y, wide)
        row = iota(at, 1)
        some = pl.ds(first, count)
        above = jnp.broadcast_to(yrecv[step, x // deep, 0, some, pl.ds(x % deep, 1), :], at)
        below = jnp.broadcast_to(yrecv[step, x // deep, 1, some, pl.ds(x % deep, 1), :], at)
        up = jnp.where(row == Y - 1, above, pltpu.roll(value, Y - 1, 1))
        down = jnp.where(row == 0, below, pltpu.roll(value, 1, 1))
        return up, down

    keep.wait()
    for c in order:
        for d in range(len(peers)):
            arriving[c, d].wait_recv()
        exchange(0, c)

    leaving = []

    def leave(c):
        rows = pl.ds(c * piece, piece)
        out_rows = part_of(group, c)
        for d, peer in enumerate(peers):
            pairs = (
                (final.at[pl.ds(peer * own, own), rows, :], tracers_out.at[:, out_rows, :]),
                (final.at[tracers, rows, :], heat_out.at[out_rows, :]),
            )
            for i, (source_ref, target_ref) in enumerate(pairs):
                copy = pltpu.make_async_remote_copy(
                    src_ref=source_ref,
                    dst_ref=target_ref,
                    send_sem=out_send.at[d, c, i],
                    recv_sem=out_recv.at[d, c, i],
                    device_id={"tracer": peer},
                    device_id_type=MESH,
                )
                copy.start()
                leaving.append(copy)
        pairs = (
            (final.at[slot, rows, :], tracers_out.at[:, out_rows, :]),
            (final.at[tracers, rows, :], heat_out.at[out_rows, :]),
        )
        for i, (source_ref, target_ref) in enumerate(pairs):
            copy = pltpu.make_async_copy(source_ref, target_ref, local_sem.at[c, 1 + i])
            copy.start()
            leaving.append(copy)

    def advance(step, c):
        columns, heats, wets = [], [], []
        for x in range(c * deep, (c + 1) * deep):
            here = pl.ds((x + 1) * Y, Y)
            ahead = pl.ds((x + 2) * Y, Y)
            behind = pl.ds(x * Y, Y)
            cell = pl.ds(x * Y, Y)
            if step == 0:
                speed_wet = state[0, pl.ds(fields + 1, 2), here, :]
                up, down = beside_y(0, speed_wet, x, fields + 1, 2)
                wet = speed_wet[1]
                east = state[0, fields, here, :] * wet * state[0, fields + 2, ahead, :]
                west = state[0, fields, behind, :] * state[0, fields + 2, behind, :] * wet
                north = speed_wet[0] * wet * up[1]
                south = down[0] * down[1] * wet
                scaled = TIME_STEP * wet
                coef[0, cell, :] = wet - scaled * (
                    jnp.maximum(east, 0.0) - jnp.minimum(west, 0.0)
                    + jnp.maximum(north, 0.0) - jnp.minimum(south, 0.0)
                )
                coef[1, cell, :] = -scaled * jnp.minimum(east, 0.0)
                coef[2, cell, :] = scaled * jnp.maximum(west, 0.0)
                coef[3, cell, :] = -scaled * jnp.minimum(north, 0.0)
                coef[4, cell, :] = scaled * jnp.maximum(south, 0.0)
            value = state[step, pl.ds(0, fields), here, :]
            up, down = beside_y(step, value, x, 0, fields)
            moved = (
                coef[0, cell, :] * value
                + coef[1, cell, :] * state[step, pl.ds(0, fields), ahead, :]
                + coef[2, cell, :] * state[step, pl.ds(0, fields), behind, :]
                + coef[3, cell, :] * up
                + coef[4, cell, :] * down
            )
            columns.append(moved[:tracers].reshape(tracers * Y, wide))
            heats.append(moved[tracers])
            wets.append(state[0, fields + 2, here, :])
        mixed = jnp.concatenate(columns, axis=1)
        parts = halves(mixed)
        ahead_rows = dot3(head, parts)
        result = dot3(four, parts)
        rates = []
        for sub in range(SUB):
            if sub == 0:
                rows = mixed[: 3 * Y]
            else:
                rows = ahead_rows[(sub - 1) * 3 * Y : sub * 3 * Y]
                for i, rate in enumerate(rates):
                    rows = rows + source[sub - 1 - i] * jnp.concatenate([rate] * 3, axis=0)
            nutrient, chl, phyto = rows[:Y], rows[Y : 2 * Y], rows[2 * Y :]
            shade = unstack(light(jnp.abs(stack(chl, wide))), Y)
            rates.append(
                GROWTH_MAX * shade * nutrient / (jnp.abs(nutrient) + HALF_SAT) * phyto
            )
        result = result + dot3(inject, halves(jnp.concatenate(rates, axis=0)))
        chl_abs = jnp.abs(stack(result[Y : 2 * Y], wide))
        heating = HEAT_GAIN * chl_abs * light(chl_abs)
        heat = jnp.concatenate(heats, axis=0) + TIME_STEP * jnp.concatenate(wets, axis=0) * heating
        if step < STEPS - 1:
            target, base = state.at[step + 1], Y + c * piece
        else:
            target, base = final, c * piece
        for x in range(deep):
            target[pl.ds(0, tracers), pl.ds(base + x * Y, Y), :] = result[
                :, x * wide : (x + 1) * wide
            ].reshape(tracers, Y, wide)
        target[tracers, pl.ds(base, piece), :] = heat

    for step in range(STEPS):
        for c in order:
            for side in (NORTH, SOUTH):
                halos[step, c, side].wait_recv()
            if c == 0:
                halos[step, chunks - 1, EAST].wait_recv()
            if c == chunks - 1:
                halos[step, 0, WEST].wait_recv()
            advance(step, c)
            if step < STEPS - 1:
                exchange(step + 1, c)
            else:
                leave(c)
    for copy in leaving:
        copy.wait()
    for copy in sent + list(arriving.values()):
        copy.wait_send()

SHARE = 5
FIRST = 3


def wide_halves(x):
    high, low = halves(x)
    return jnp.concatenate([high, high, low], axis=1)


def tall_halves(x):
    high, low = halves(x)
    return jnp.concatenate([high, low, high], axis=0)


def pair_tables(rates_ref, yields_ref, tracers, wide, Y):
    rows = tracers * Y
    spread = (iota((rows, tracers), 0) // Y == iota((rows, tracers), 1)).astype(jnp.float32)
    same = iota((rows, rows), 0) % Y == iota((rows, rows), 1) % Y
    full = exact_dot(exact_dot(spread, rates_ref[...]), spread, ((1,), (1,)))
    full = jnp.where(same, full, 0.0) * REACT_STEP
    diagonal = (iota((rows, rows), 0) == iota((rows, rows), 1)).astype(jnp.float32)
    one = diagonal + full
    two = exact_dot(one, one)
    three = exact_dot(two, one)
    four = exact_dot(two, two)
    source = [
        exact_dot(spread * yields_ref[...], jnp.ones((tracers, wide), jnp.float32)) * REACT_STEP
    ]
    for power in (one, two, three):
        source.append(exact_dot(power, source[0]))
    powers = jnp.concatenate([power[: 3 * Y] for power in (one, two, three)] + [four], axis=0)
    shape = (rows, wide)
    lane = iota(shape, 1)
    inject = jnp.zeros(shape, jnp.float32)
    for sub in range(SUB):
        hit = jnp.logical_and(lane // Y == sub, lane % Y == iota(shape, 0) % Y)
        inject = inject + jnp.where(hit, source[SUB - 1 - sub], 0.0)
    return (
        wide_halves(powers),
        wide_halves(inject[:, : SUB * Y]),
        [v[: 3 * Y] for v in source],
    )


def pair_plan(half):
    low = -SHARE - STEPS
    ranges = [(half - STEPS, STEPS)]
    for at, end in ((SHARE - STEPS, half - STEPS), (low, SHARE - STEPS)):
        while at < end:
            size = min(STEPS, end - at)
            ranges.append((at, size))
            at += size
    return low, ranges


def pair_kernel(
    regions, sects,
    solute, heat_hbm, east_hbm, north_hbm, layers_hbm, rates_hbm, yields_hbm,
    tracers_out, heat_out,
    layers_in, rates_ref, yields_ref, state, coef, wets, final, measure,
    send_sem, recv_sem, go_sem,
):
    groups = 2
    region, group, sect = (lax.axis_index(a) for a in ("region", "tracer", "sect"))
    own, X, Y, wide = solute.shape
    half = X // groups
    tracers = own * groups
    fields = tracers + 1
    base = STEPS + 1
    low, ranges = pair_plan(half)
    reach = half - low
    odd = region % 2
    part = group + odd * (1 - 2 * group)
    peer = 1 - group

    def pick(flag, a, b):
        return a + flag * (b - a)

    def P(u, k, flag=part):
        return pick(flag, half + STEPS - u - k, u - low)

    def B(u, k, flag=part):
        return pick(flag, half - u - k, half + u)

    outer_region = lax.rem(region + pick(part, regions - 1, 1), regions)
    outer_part = 1 - part
    outer_odd = outer_region % 2
    beside = {"region": outer_region, "tracer": outer_part + outer_odd * (1 - 2 * outer_part)}
    north = {"sect": lax.rem(sect + 1, sects)}
    south = {"sect": lax.rem(sect + sects - 1, sects)}
    across = {"tracer": peer}
    mine, other = pl.ds(group * own, own), pl.ds(peer * own, own)

    names, lines = {}, {}

    def slot(name):
        return names.setdefault(name, len(names))

    def tally(name, ref):
        lines[name] = lines.get(name, 0) + math.prod(ref.shape) // wide

    def settle(name, sems=recv_sem):
        some = measure.at[pl.ds(0, lines[name])]
        at = slot(name) if sems is recv_sem else int(name[4:])
        with jax.named_scope(name):
            pltpu.make_async_copy(some, some, sems.at[at]).wait()

    def local(name, source_ref, target_ref):
        tally(name, target_ref)
        pltpu.make_async_copy(source_ref, target_ref, recv_sem.at[slot(name)]).start()

    def remote(name, source_ref, target_ref, device, turn=0):
        tally(name, target_ref)
        tally(f"sent{turn}", source_ref)
        push(name, source_ref, target_ref, device, turn)

    def push(name, source_ref, target_ref, device, turn=0):
        pltpu.make_async_remote_copy(
            src_ref=source_ref,
            dst_ref=target_ref,
            send_sem=send_sem.at[turn],
            recv_sem=recv_sem.at[slot(name)],
            device_id=device,
            device_id_type=MESH,
        ).start()

    raw = state.at[0]
    body = pl.ds(base, Y)
    blank = jnp.zeros((tracers + 4, 1, STEPS, wide), jnp.float32)
    for u in (low, half, half + 1, half + 2):
        for row in (base - STEPS, base + Y):
            raw[:, pl.ds(P(u, 1), 1), pl.ds(row, STEPS), :] = blank
    barrier = pltpu.get_barrier_semaphore()
    @pl.when(part == 0)
    def _():
        pl.semaphore_signal(barrier, inc=1, device_id=beside, device_id_type=MESH)

    for device in (across, north, south):
        pl.semaphore_signal(barrier, inc=1, device_id=device, device_id_type=MESH)

    small = [
        pltpu.make_async_copy(source_ref, target_ref, recv_sem.at[slot(f"small{i}")])
        for i, (source_ref, target_ref) in enumerate(
            ((layers_hbm, layers_in), (rates_hbm, rates_ref), (yields_hbm, yields_ref))
        )
    ]
    for copy in small:
        copy.start()
    p_all, b_all = P(low, reach), B(low, reach)
    in_block = pl.ds(b_all, reach)
    in_state = pl.ds(p_all, reach)
    extra = ((heat_hbm, tracers), (east_hbm, fields), (north_hbm, fields + 1))
    local("loads", solute.at[:, in_block], raw.at[mine, in_state, body])
    for ref, field in extra:
        local("loads", ref.at[in_block], raw.at[field, in_state, body])

    with jax.named_scope("barrier"):
        pl.semaphore_wait(barrier, 3 + part)

    def cross(i):
        u, k = ranges[i]
        remote(
            f"x{i}",
            solute.at[:, pl.ds(B(u, k, 1 - part), k)],
            raw.at[mine, pl.ds(P(u, k, 1 - part), k), body],
            across,
        )

    edge = half - STEPS
    edge_block = pl.ds(B(edge, STEPS), STEPS)
    edge_state = pl.ds(P(edge, STEPS), STEPS)
    past = pl.ds(pick(part, reach, 0), STEPS)
    cross(0)
    edges = [(solute.at[:, edge_block], raw.at[mine, past, body])]
    edges += [(ref.at[edge_block], raw.at[field, past, body]) for ref, field in extra]
    for source_ref, target_ref in edges:
        tally("outer", target_ref)
        tally("sent0", source_ref)

    @pl.when(part == 1)
    def _():
        pl.semaphore_signal(go_sem, inc=1, device_id=beside, device_id_type=MESH)
        for source_ref, target_ref in edges:
            push("outer", source_ref, target_ref, beside)

    for i in range(1, len(ranges)):
        cross(i)
    far = sect % 2

    def both_sides(send):
        for first in (0, 1):
            @pl.when(far == first)
            def _():
                for side in (first, 1 - first):
                    send(side, (south, north)[side])

    def halo_row(side, deep=STEPS):
        return pl.ds(base - deep if side else base + Y, deep)

    def tally_sides(name, refs):
        for ref in refs:
            for _ in range(2):
                tally(name, ref)
                tally("sent0", ref)

    def direct_rows(name, u, k):
        b, p = pl.ds(B(u, k), k), pl.ds(P(u, k), k)
        refs = [(solute.at[:, b], mine)] + [(ref.at[b], field) for ref, field in extra]

        def send(side, device):
            block_rows = pl.ds(Y - STEPS if side else 0, STEPS)
            for ref, field in refs:
                rows = ref.at[:, :, block_rows] if ref is refs[0][0] else ref.at[:, block_rows]
                push(name, rows, raw.at[field, p, halo_row(side)], device)

        both_sides(send)
        tally_sides(name, [raw.at[field, p, halo_row(0)] for _, field in refs])

    def beside_rows(name, some, u, k, deep=STEPS):
        place = pl.ds(P(u, k), k)

        def send(side, device):
            start = base + Y - deep if side else base
            push(
                name,
                raw.at[some, place, pl.ds(start, deep)],
                raw.at[some, place, halo_row(side, deep)],
                device,
            )

        both_sides(send)
        tally_sides(name, [raw.at[some, place, halo_row(0, deep)]])

    near = 1 + -(-(FIRST + 2 * STEPS) // STEPS)
    cone = min((near - 1) * STEPS, edge + STEPS + STEPS - SHARE)
    cone_at = max(low + 1, SHARE - STEPS)
    cone_end = SHARE - STEPS + cone
    direct_rows("rows", cone_at, cone_end - cone_at)
    if cone_end < half:
        direct_rows("rest", cone_end, half - cone_end)

    for copy in small:
        copy.wait()
    total = X * Y
    pick_rows = iota((total, X), 0) // Y == iota((total, X), 1)
    depth = lax.dot_general(
        pick_rows.astype(jnp.bfloat16),
        layers_in[...].astype(jnp.float32).astype(jnp.bfloat16),
        (((1,), (1,)), ((), ())),
        preferred_element_type=jnp.float32,
    )
    depth = jnp.where(iota((total, Y), 0) % Y == iota((total, Y), 1), depth, 0.0)
    depth = half_dot(depth.astype(jnp.bfloat16), jnp.ones((Y, wide), jnp.bfloat16))
    wets[...] = (iota((total, wide), 1).astype(jnp.float32) < depth).astype(jnp.float32).reshape(
        X, Y, wide
    )
    wet_field = fields + 2
    raw[wet_field, in_state, body, :] = wets[in_block]
    beside_rows("rows", pl.ds(wet_field, 1), low + 1, reach - 1)

    with jax.named_scope("make_tables"):
        powers, inject, source = pair_tables(rates_ref, yields_ref, tracers, wide, Y)
    @pl.when(part == 0)
    def _():
        pl.semaphore_wait(go_sem, 1)
        for source_ref, target_ref in edges:
            push("outer", source_ref, target_ref, beside)

    remote("outer", raw.at[wet_field, edge_state, body], raw.at[wet_field, past, body], beside)
    shape = (wide, wide)
    upper = (iota(shape, 0) < iota(shape, 1)).astype(jnp.float32)
    upper = upper + 0.5 * (iota(shape, 0) == iota(shape, 1)).astype(jnp.float32)
    upper = jnp.concatenate([upper.astype(jnp.bfloat16)] * 2, axis=0)
    level = (iota((Y, wide), 1).astype(jnp.float32) + 0.5) * (-WATER_ATT / wide)
    settle("loads")

    def light(chl_abs):
        high, low_part = halves(chl_abs)
        above = half_dot(jnp.concatenate([high, low_part], axis=1), upper)
        tall = jnp.concatenate([level] * (chl_abs.shape[0] // Y), axis=0)
        return jnp.exp(tall - CHL_ATT / wide * above)

    done = set()

    def once(name):
        fresh = name not in done
        done.add(name)
        return fresh

    def arrive(i):
        if once(f"x{i}"):
            settle(f"x{i}")
            u, k = ranges[i]
            some = pl.ds(P(u, k), k)
            if i == 0:
                remote("outer", raw.at[other, some, body], raw.at[other, past, body], beside)
            skip = int(u == low)
            beside_rows(f"y{i}", other, u + skip, k - skip)
            if i == near - 1 and low + 1 < cone_at:
                direct_rows("inner", low + 1, cone_at - low - 1)

    def arrive_outer():
        arrive(0)
        if once("outer"):
            settle("outer")
            beside_rows("corner", slice(None), half, STEPS - 1, STEPS - 1)

    def ready(first, last):
        if once("rows"):
            settle("rows")
        for name, wanted in (("inner", first < cone_at), ("rest", last >= cone_end)):
            if wanted and name in lines and once(name):
                settle(name)
        for i, (u, k) in enumerate(ranges):
            if u <= last and first < u + k:
                arrive(i)
                if once(f"y{i}"):
                    settle(f"y{i}")
        if last >= half:
            arrive_outer()
            if once("corner"):
                settle("corner")

    windows = [
        (base - STEPS + 1, base + Y + STEPS - 1 - Y),
        (base - 1, base + 1),
        (base,),
    ]

    def stencil(step, p, r):
        here = pl.ds(r, Y)
        up_rows, down_rows = pl.ds(r + 1, Y), pl.ds(r - 1, Y)
        if step == 0:
            wet = raw[wet_field, p, here, :]
            south_wet = raw[wet_field, p, down_rows, :]
            east = raw[fields, p, here, :] * wet * raw[wet_field, p + 1, here, :]
            west = raw[fields, p - 1, here, :] * raw[wet_field, p - 1, here, :] * wet
            up = raw[fields + 1, p, here, :] * wet * raw[wet_field, p, up_rows, :]
            down = raw[fields + 1, p, down_rows, :] * south_wet * wet
            scaled = TIME_STEP * wet
            c = [
                wet
                - scaled
                * (
                    jnp.maximum(east, 0.0) - jnp.minimum(west, 0.0)
                    + jnp.maximum(up, 0.0) - jnp.minimum(down, 0.0)
                ),
                -scaled * jnp.minimum(east, 0.0),
                scaled * jnp.maximum(west, 0.0),
                -scaled * jnp.minimum(up, 0.0),
                scaled * jnp.maximum(down, 0.0),
                scaled,
            ]
            for i, v in enumerate(c):
                coef[i, p, here, :] = v
        else:
            c = [coef[i, p, here, :] for i in range(6)]
        some = pl.ds(0, fields)
        moved = (
            c[0] * state[step, some, p, here, :]
            + c[1] * state[step, some, p + 1, here, :]
            + c[2] * state[step, some, p - 1, here, :]
            + c[3] * state[step, some, p, up_rows, :]
            + c[4] * state[step, some, p, down_rows, :]
        )
        return moved, c[5]

    def advance(*work):
        work = [item for item in work if item[2] > 0]
        for step, u, k in work:
            if step == 0:
                ready(u - 1, u + k)
        with jax.named_scope("go" + "_".join(f"{s}:{u}:{k}" for s, u, k in work)):
            compute(work)

    def compute(work):
        tiles = []
        for step, u, k in work:
            p = P(u, k)
            for i in range(k):
                for r in windows[step]:
                    tiles.append((step, p + i, r))
        columns, heats, scales = [], [], []
        for step, p, r in tiles:
            moved, scaled = stencil(step, p, r)
            columns.append(moved[:tracers].reshape(tracers * Y, wide))
            heats.append(moved[tracers])
            scales.append(scaled)
        n = len(tiles)
        mixed = jnp.concatenate(columns, axis=1)
        ahead = half_dot(powers, tall_halves(mixed))
        block = 3 * Y
        result = ahead[3 * block :]

        def part_of(rows, i):
            return stack(rows[i * Y : (i + 1) * Y], wide)

        def spread(v, i):
            return jnp.concatenate([v[i * Y : (i + 1) * Y]] * n, axis=0)

        rates = []
        for sub in range(SUB):
            rows = mixed[:block] if sub == 0 else ahead[(sub - 1) * block : sub * block]
            value = []
            for i in range(3):
                v = part_of(rows, i)
                for j, rate in enumerate(rates):
                    v = v + spread(source[sub - 1 - j], i) * rate
                value.append(v)
            nutrient, chl, phyto = value
            rates.append(
                light(jnp.abs(chl)) * (nutrient / (jnp.abs(nutrient) + HALF_SAT) * phyto)
            )
        chl = part_of(result, 1)
        for j, rate in enumerate(rates):
            chl = chl + spread(source[SUB - 1 - j], 1) * rate
        chl_abs = jnp.abs(chl)
        flat = jnp.concatenate([unstack(rate, Y) for rate in rates], axis=0)
        result = result + half_dot(inject, tall_halves(flat))
        heat = jnp.concatenate(heats, axis=0) + HEAT_GAIN * (
            jnp.concatenate(scales, axis=0) * chl_abs * light(chl_abs)
        )
        for i, (step, p, r) in enumerate(tiles):
            value = result[:, i * wide : (i + 1) * wide].reshape(tracers, Y, wide)
            if step < STEPS - 1:
                here = pl.ds(r, Y)
                state[step + 1, pl.ds(0, tracers), p, here, :] = value
                state[step + 1, tracers, p, here, :] = heat[i * Y : (i + 1) * Y]
            else:
                final[pl.ds(0, tracers), p, :, :] = value
                final[tracers, p, :, :] = heat[i * Y : (i + 1) * Y]

    def leave(u, k):
        if k <= 0:
            return
        some, place = pl.ds(P(u, k), k), pl.ds(B(u, k), k)
        if u >= SHARE:
            remote("arrivals", final.at[other, some], tracers_out.at[:, place], across, 1)
            remote("arrivals", final.at[tracers, some], heat_out.at[place], across, 1)
        local("leaving", final.at[mine, some], tracers_out.at[:, place])
        local("leaving", final.at[tracers, some], heat_out.at[place])

    for action in schedule(half):
        if action[0] == "x":
            arrive(action[1])
        elif action[0] == "z":
            arrive_outer()
        elif action[0] == "go":
            advance(*action[1:])
        else:
            leave(*action[1:])
    settle("leaving")
    settle("arrivals")
    settle("sent0", send_sem)
    settle("sent1", send_sem)


def schedule(half):
    count = len(pair_plan(half)[1])
    h, a, b = SHARE, FIRST, half - STEPS
    near = 1 + -(-(a + 2 * STEPS) // STEPS)
    inner = [[(s, -h - 2 + s, 2 * h)] if h else [] for s in range(STEPS)]
    own = 1 + -(-(b - h + STEPS) // STEPS)
    rest = b - h - a
    late = [("x", i) for i in range(own, count)]
    plan = [("x", i) for i in range(own)]
    plan += [("go", (0, h - 2, a + 4)), ("z",), *late[:1], ("go", (1, h - 1, a + 2)), *late[1:2]]
    plan += [("go", (2, h, a), (0, h + a + 2, rest)), ("out", h, a)]
    plan += [*late[2:], ("go", (1, h + a + 1, rest), (0, b + 2, 3))]
    plan += [("go", (2, h + a, rest), (1, b + 1, 3)), ("out", h + a, rest)]
    plan += [("go", (2, b, 3)), ("out", b, 3)]
    for s in range(STEPS if h else 0):
        plan.append(("go", *inner[s]))
    return plan + ([("out", -h, 2 * h)] if h else [])


def paired(shape, groups, regions, sects):
    return (
        groups == 2 and regions > 1 and regions % 2 == 0 and sects > 1
        and shape[2] == 8 and shape[3] == 128 and shape[1] % 2 == 0 and shape[1] >= 24
        and shape[0] * groups * shape[2] == 128
    )


def write_out(mixture, heat, mixture_out, heat_out, sems):
    own = mixture.shape[0]
    copies = [
        pltpu.make_async_copy(mixture.at[i], mixture_out.at[i], sems.at[i]) for i in range(own)
    ]
    copies.append(pltpu.make_async_copy(heat, heat_out, sems.at[own]))
    for copy in copies:
        copy.start()
    for copy in copies:
        copy.wait()


def pair_call(solute, thermal, eastward, northward, layers, rates, yields, regions, sects):
    own, X, Y, wide = solute.shape
    tracers = own * 2
    half = X // 2
    low, ranges = pair_plan(half)
    columns = half - low + STEPS
    operands = [
        pltpu.with_memory_space_constraint(v, pltpu.HBM)
        for v in (solute, thermal, eastward, northward, layers.T, rates, yields.reshape(1, tracers))
    ]
    hbm = pl.BlockSpec(memory_space=pltpu.HBM)
    free = pl.BlockSpec(memory_space=pl.ANY)
    dma = pltpu.SemaphoreType.DMA
    mixture, heat = pl.pallas_call(
        functools.partial(pair_kernel, regions, sects),
        out_shape=(
            jax.ShapeDtypeStruct(solute.shape, jnp.float32),
            jax.ShapeDtypeStruct(thermal.shape, jnp.float32),
        ),
        in_specs=[hbm] * 7,
        out_specs=(free, free),
        scratch_shapes=[
            pltpu.VMEM((Y, X), jnp.int32),
            pltpu.VMEM((tracers, tracers), jnp.float32),
            pltpu.VMEM((1, tracers), jnp.float32),
            pltpu.VMEM((STEPS, tracers + 4, columns, 2 * Y, wide), jnp.float32),
            pltpu.VMEM((6, columns, 2 * Y, wide), jnp.float32),
            pltpu.VMEM((X, Y, wide), jnp.float32),
            pltpu.VMEM((tracers + 1, columns, Y, wide), jnp.float32),
            pltpu.VMEM((MEASURE, wide), jnp.float32),
            dma((2,)),
            dma((len(ranges) * 2 + 11,)),
            pltpu.SemaphoreType.REGULAR,
        ],
        compiler_params=pltpu.CompilerParams(
            collective_id=0, has_side_effects=True, vmem_limit_bytes=40 << 20
        ),
    )(*operands)
    return pl.pallas_call(
        write_out,
        out_shape=(
            jax.ShapeDtypeStruct(solute.shape, jnp.float32),
            jax.ShapeDtypeStruct(thermal.shape, jnp.float32),
        ),
        in_specs=[free] * 2,
        out_specs=(hbm, hbm),
        scratch_shapes=[dma((own + 1,))],
        compiler_params=pltpu.CompilerParams(vmem_limit_bytes=1 << 20),
    )(mixture, heat)


MEASURE = 8192


def solution(mesh):
    regions, groups, sects = (mesh.shape[a] for a in ("region", "tracer", "sect"))

    def body(solute, thermal, eastward, northward, layers, rates, yields):
        if paired(solute.shape, groups, regions, sects):
            return pair_call(
                solute, thermal, eastward, northward, layers, rates, yields, regions, sects
            )
        own, rows, cols, wide = solute.shape
        tracers = own * groups
        span = rows // groups
        fields = tracers + 1
        flat = (rows * cols, wide)
        free, hbm = pl.BlockSpec(memory_space=pl.ANY), pl.BlockSpec(memory_space=pltpu.HBM)
        dma = pltpu.SemaphoreType.DMA
        peers = max(groups - 1, 1)
        chunks = plan(span)[0]
        mixture, heat = pl.pallas_call(
            functools.partial(kernel, regions, groups, sects),
            out_shape=(
                jax.ShapeDtypeStruct((own, *flat), jnp.float32),
                jax.ShapeDtypeStruct(flat, jnp.float32),
            ),
            in_specs=[hbm] * 7,
            out_specs=(free, free),
            scratch_shapes=[
                pltpu.VMEM((cols, rows), jnp.int32),
                pltpu.VMEM((tracers, tracers), jnp.float32),
                pltpu.VMEM((1, tracers), jnp.float32),
                pltpu.VMEM((STEPS, fields + 3, (span + 2) * cols, wide), jnp.float32),
                pltpu.VMEM((STEPS, chunks, 2, fields + 3, span // chunks, wide), jnp.float32),
                pltpu.VMEM((STEPS, chunks, 2, fields + 3, span // chunks, wide), jnp.float32),
                pltpu.VMEM((6, *flat), jnp.float32),
                pltpu.VMEM((fields, span * cols, wide), jnp.float32),
                dma((peers, chunks)),
                dma((peers, chunks)),
                dma((STEPS, chunks, 4)),
                dma((STEPS, chunks, 4)),
                dma((peers, chunks, 2)),
                dma((peers, chunks, 2)),
                dma((chunks, 3)),
                dma((6,)),
            ],
            compiler_params=pltpu.CompilerParams(
                collective_id=0, has_side_effects=True, vmem_limit_bytes=60 << 20
            ),
        )(
            solute.reshape(own, *flat),
            thermal.reshape(flat),
            eastward.reshape(flat),
            northward.reshape(flat),
            layers.T,
            rates,
            yields.reshape(1, tracers),
        )
        return mixture.reshape(solute.shape), heat.reshape(thermal.shape)

    return jax.shard_map(
        body,
        mesh=mesh,
        in_specs=(
            P("tracer", "region", "sect", None),
            P("region", "sect", None),
            P("region", "sect", None),
            P("region", "sect", None),
            P("region", "sect"),
            P(),
            P(),
        ),
        out_specs=(P("tracer", "region", "sect", None), P("region", "sect", None)),
        check_vma=False,
    )
```

```python
import functools
import math

import jax
import jax.numpy as jnp
from jax import lax
from jax.experimental import pallas as pl
from jax.experimental.pallas import tpu as pltpu
from jax.sharding import PartitionSpec as P

STEPS = 3
SUB = 4

TIME_STEP = 0.2
REACT_STEP = 0.1
GROWTH_MAX = 1.0
HALF_SAT = 0.5
WATER_ATT = 3.0
CHL_ATT = 2.0
HEAT_GAIN = 0.5

MESH = pl.DeviceIdType.MESH
HIGHEST = lax.Precision.HIGHEST
EAST, WEST, NORTH, SOUTH = range(4)


def iota(shape, dim):
    return lax.broadcasted_iota(jnp.int32, shape, dim)


def exact_dot(a, b, dims=((1,), (0,))):
    return lax.dot_general(
        a, b, (dims, ((), ())), precision=HIGHEST, preferred_element_type=jnp.float32
    )


def halves(x):
    high = x.astype(jnp.bfloat16)
    return high, (x - high.astype(jnp.float32)).astype(jnp.bfloat16)


def half_dot(a, b):
    return jnp.dot(a, b, preferred_element_type=jnp.float32)


def dot3(a, b):
    return half_dot(a[0], b[0]) + half_dot(a[1], b[0]) + half_dot(a[0], b[1])


def tables(rates_ref, yields_ref, tracers, wide, Y):
    rows = tracers * Y
    spread = (iota((rows, tracers), 0) // Y == iota((rows, tracers), 1)).astype(jnp.float32)
    same = iota((rows, rows), 0) % Y == iota((rows, rows), 1) % Y
    full = exact_dot(exact_dot(spread, rates_ref[...]), spread, ((1,), (1,)))
    full = jnp.where(same, full, 0.0) * REACT_STEP
    diagonal = (iota((rows, rows), 0) == iota((rows, rows), 1)).astype(jnp.float32)
    one = diagonal + full
    two = exact_dot(one, one)
    three = exact_dot(two, one)
    four = exact_dot(two, two)
    source = [
        exact_dot(spread * yields_ref[...], jnp.ones((tracers, wide), jnp.float32)) * REACT_STEP
    ]
    for power in (one, two, three):
        source.append(exact_dot(power, source[0]))
    head = jnp.concatenate([power[: 3 * Y] for power in (one, two, three)], axis=0)
    shape = (rows, wide)
    lane = iota(shape, 1)
    inject = jnp.zeros(shape, jnp.float32)
    for sub in range(SUB):
        hit = jnp.logical_and(lane // Y == sub, lane % Y == iota(shape, 0) % Y)
        inject = inject + jnp.where(hit, source[SUB - 1 - sub], 0.0)
    return head, four, inject[:, : SUB * Y], [v[: 3 * Y] for v in source[: SUB - 1]]


def stack(flat, wide):
    return jnp.concatenate(
        [flat[:, i * wide : (i + 1) * wide] for i in range(flat.shape[1] // wide)], axis=0
    )


def unstack(tall, Y):
    return jnp.concatenate(
        [tall[i * Y : (i + 1) * Y] for i in range(tall.shape[0] // Y)], axis=1
    )


def plan(span):
    return (3, (0, 2, 1)) if span % 3 == 0 else (1, (0,))


def kernel(
    regions, groups, sects,
    solute, heat_hbm, east_hbm, north_hbm, layers_hbm, rates_hbm, yields_hbm,
    tracers_out, heat_out,
    layers_in, rates_ref, yields_ref,
    state, ysend, yrecv, coef, final,
    in_send, in_recv, halo_send, halo_recv, out_send, out_recv, local_sem, load_sem,
):
    region, group, sect = (lax.axis_index(a) for a in ("region", "tracer", "sect"))
    own, wide, Y = solute.shape[0], solute.shape[2], layers_in.shape[0]
    tracers = own * groups
    block = heat_hbm.shape[0] // groups
    span = block // Y
    fields = tracers + 1
    every = fields + 3

    def place(reg, t):
        return t + (reg % 2) * (groups - 1 - 2 * t)

    part = place(region, group)
    last = groups - 1
    next_region = lax.rem(region + 1, regions)
    past_region = lax.rem(region + regions - 1, regions)
    east_region = jnp.where(part == last, next_region, region)
    west_region = jnp.where(part == 0, past_region, region)
    east_part = jnp.where(part == last, 0, part + 1)
    west_part = jnp.where(part == 0, last, part - 1)
    beside = {
        EAST: {"region": east_region, "tracer": place(east_region, east_part)},
        WEST: {"region": west_region, "tracer": place(west_region, west_part)},
        NORTH: {"sect": lax.rem(sect + 1, sects)},
        SOUTH: {"sect": lax.rem(sect + sects - 1, sects)},
    }
    peers = [lax.rem(group + d, groups) for d in range(1, groups)]

    def rows_of(t):
        return pl.ds(pl.multiple_of(place(region, t) * block, Y), block)

    mine = rows_of(group)
    slot = pl.ds(group * own, own)
    inner = pl.ds(Y, block)

    barrier = pltpu.get_barrier_semaphore()
    for peer in peers:
        pl.semaphore_signal(barrier, inc=1, device_id={"tracer": peer}, device_id_type=MESH)
    for side in range(4):
        pl.semaphore_signal(barrier, inc=1, device_id=beside[side], device_id_type=MESH)
    keep = pltpu.make_async_copy(
        solute.at[:, mine, :], state.at[0, slot, inner, :], local_sem.at[0, 0]
    )
    keep.start()
    loads = []
    for i, (source_ref, target_ref) in enumerate(
        (
            (layers_hbm, layers_in),
            (rates_hbm, rates_ref),
            (yields_hbm, yields_ref),
            (heat_hbm.at[mine, :], state.at[0, tracers, inner, :]),
            (east_hbm.at[mine, :], state.at[0, fields, inner, :]),
            (north_hbm.at[mine, :], state.at[0, fields + 1, inner, :]),
        )
    ):
        copy = pltpu.make_async_copy(source_ref, target_ref, load_sem.at[i])
        copy.start()
        loads.append(copy)
    pl.semaphore_wait(barrier, groups - 1 + 4)

    chunks, order = plan(span)
    deep = span // chunks
    piece = deep * Y

    def part_of(t, c):
        return pl.ds(pl.multiple_of(place(region, t) * block + c * piece, Y), piece)

    arriving = {}
    for i, c in enumerate(order):
        for d, peer in enumerate(peers):
            copy = pltpu.make_async_remote_copy(
                src_ref=solute.at[:, part_of(peer, c), :],
                dst_ref=state.at[0, slot, pl.ds(Y + c * piece, piece), :],
                send_sem=in_send.at[d, c],
                recv_sem=in_recv.at[d, c],
                device_id={"tracer": peer},
                device_id_type=MESH,
            )
            copy.start()
            arriving[c, d] = copy

    for copy in loads:
        copy.wait()
    total = layers_in.shape[1] * Y
    pick = (iota((total, layers_in.shape[1]), 0) // Y == iota((total, layers_in.shape[1]), 1))
    depth = lax.dot_general(
        pick.astype(jnp.bfloat16),
        layers_in[...].astype(jnp.float32).astype(jnp.bfloat16),
        (((1,), (1,)), ((), ())),
        preferred_element_type=jnp.float32,
    )
    depth = jnp.where(iota((total, Y), 0) % Y == iota((total, Y), 1), depth, 0.0)
    depth = half_dot(depth.astype(jnp.bfloat16), jnp.ones((Y, wide), jnp.bfloat16))
    coef[5] = (iota((total, wide), 1).astype(jnp.float32) < depth).astype(jnp.float32)
    state[0, fields + 2, inner, :] = coef[5, mine, :]

    head, four, inject, source = tables(rates_ref, yields_ref, tracers, wide, Y)
    head, four, inject = halves(head), halves(four), halves(inject)
    upper = (iota((wide, wide), 0) < iota((wide, wide), 1)).astype(jnp.bfloat16)
    level = iota((piece, wide), 1).astype(jnp.float32) + 0.5
    tile = (1, deep)
    source = [jnp.tile(v, tile) for v in source]

    def light(chl_abs):
        high, low = halves(chl_abs)
        above = half_dot(high, upper) + half_dot(low, upper)
        return jnp.exp(
            -(WATER_ATT / wide * level + CHL_ATT / wide * (above + 0.5 * chl_abs))
        )

    sent = []

    def exchange(step, c):
        count = every if step == 0 else fields
        some = pl.ds(0, count)
        moves = {}
        if c == chunks - 1:
            moves[EAST] = (
                state.at[step, some, pl.ds(block, Y), :],
                state.at[step, some, pl.ds(0, Y), :],
            )
        if c == 0:
            moves[WEST] = (
                state.at[step, some, pl.ds(Y, Y), :],
                state.at[step, some, pl.ds(block + Y, Y), :],
            )

        def send(moves):
            for side, (source_ref, target_ref) in moves.items():
                copy = pltpu.make_async_remote_copy(
                    src_ref=source_ref,
                    dst_ref=target_ref,
                    send_sem=halo_send.at[step, c, side],
                    recv_sem=halo_recv.at[step, c, side],
                    device_id=beside[side],
                    device_id_type=MESH,
                )
                copy.start()
                sent.append(copy)
                halos[step, c, side] = copy

        send(moves)
        for f in range(count):
            for side, y in ((0, 0), (1, Y - 1)):
                ysend[step, c, side, f] = state[
                    step, f, pl.ds(Y + c * piece + y, deep, stride=Y), :
                ]
        moves = {
            NORTH: (ysend.at[step, c, 1, some], yrecv.at[step, c, 1, some]),
            SOUTH: (ysend.at[step, c, 0, some], yrecv.at[step, c, 0, some]),
        }
        send(moves)

    halos = {}

    def beside_y(step, value, x, first, count):
        at = (count, Y, wide)
        row = iota(at, 1)
        some = pl.ds(first, count)
        above = jnp.broadcast_to(yrecv[step, x // deep, 0, some, pl.ds(x % deep, 1), :], at)
        below = jnp.broadcast_to(yrecv[step, x // deep, 1, some, pl.ds(x % deep, 1), :], at)
        up = jnp.where(row == Y - 1, above, pltpu.roll(value, Y - 1, 1))
        down = jnp.where(row == 0, below, pltpu.roll(value, 1, 1))
        return up, down

    keep.wait()
    for c in order:
        for d in range(len(peers)):
            arriving[c, d].wait_recv()
        exchange(0, c)

    leaving = []

    def leave(c):
        rows = pl.ds(c * piece, piece)
        out_rows = part_of(group, c)
        for d, peer in enumerate(peers):
            pairs = (
                (final.at[pl.ds(peer * own, own), rows, :], tracers_out.at[:, out_rows, :]),
                (final.at[tracers, rows, :], heat_out.at[out_rows, :]),
            )
            for i, (source_ref, target_ref) in enumerate(pairs):
                copy = pltpu.make_async_remote_copy(
                    src_ref=source_ref,
                    dst_ref=target_ref,
                    send_sem=out_send.at[d, c, i],
                    recv_sem=out_recv.at[d, c, i],
                    device_id={"tracer": peer},
                    device_id_type=MESH,
                )
                copy.start()
                leaving.append(copy)
        pairs = (
            (final.at[slot, rows, :], tracers_out.at[:, out_rows, :]),
            (final.at[tracers, rows, :], heat_out.at[out_rows, :]),
        )
        for i, (source_ref, target_ref) in enumerate(pairs):
            copy = pltpu.make_async_copy(source_ref, target_ref, local_sem.at[c, 1 + i])
            copy.start()
            leaving.append(copy)

    def advance(step, c):
        columns, heats, wets = [], [], []
        for x in range(c * deep, (c + 1) * deep):
            here = pl.ds((x + 1) * Y, Y)
            ahead = pl.ds((x + 2) * Y, Y)
            behind = pl.ds(x * Y, Y)
            cell = pl.ds(x * Y, Y)
            if step == 0:
                speed_wet = state[0, pl.ds(fields + 1, 2), here, :]
                up, down = beside_y(0, speed_wet, x, fields + 1, 2)
                wet = speed_wet[1]
                east = state[0, fields, here, :] * wet * state[0, fields + 2, ahead, :]
                west = state[0, fields, behind, :] * state[0, fields + 2, behind, :] * wet
                north = speed_wet[0] * wet * up[1]
                south = down[0] * down[1] * wet
                scaled = TIME_STEP * wet
                coef[0, cell, :] = wet - scaled * (
                    jnp.maximum(east, 0.0) - jnp.minimum(west, 0.0)
                    + jnp.maximum(north, 0.0) - jnp.minimum(south, 0.0)
                )
                coef[1, cell, :] = -scaled * jnp.minimum(east, 0.0)
                coef[2, cell, :] = scaled * jnp.maximum(west, 0.0)
                coef[3, cell, :] = -scaled * jnp.minimum(north, 0.0)
                coef[4, cell, :] = scaled * jnp.maximum(south, 0.0)
            value = state[step, pl.ds(0, fields), here, :]
            up, down = beside_y(step, value, x, 0, fields)
            moved = (
                coef[0, cell, :] * value
                + coef[1, cell, :] * state[step, pl.ds(0, fields), ahead, :]
                + coef[2, cell, :] * state[step, pl.ds(0, fields), behind, :]
                + coef[3, cell, :] * up
                + coef[4, cell, :] * down
            )
            columns.append(moved[:tracers].reshape(tracers * Y, wide))
            heats.append(moved[tracers])
            wets.append(state[0, fields + 2, here, :])
        mixed = jnp.concatenate(columns, axis=1)
        parts = halves(mixed)
        ahead_rows = dot3(head, parts)
        result = dot3(four, parts)
        rates = []
        for sub in range(SUB):
            if sub == 0:
                rows = mixed[: 3 * Y]
            else:
                rows = ahead_rows[(sub - 1) * 3 * Y : sub * 3 * Y]
                for i, rate in enumerate(rates):
                    rows = rows + source[sub - 1 - i] * jnp.concatenate([rate] * 3, axis=0)
            nutrient, chl, phyto = rows[:Y], rows[Y : 2 * Y], rows[2 * Y :]
            shade = unstack(light(jnp.abs(stack(chl, wide))), Y)
            rates.append(
                GROWTH_MAX * shade * nutrient / (jnp.abs(nutrient) + HALF_SAT) * phyto
            )
        result = result + dot3(inject, halves(jnp.concatenate(rates, axis=0)))
        chl_abs = jnp.abs(stack(result[Y : 2 * Y], wide))
        heating = HEAT_GAIN * chl_abs * light(chl_abs)
        heat = jnp.concatenate(heats, axis=0) + TIME_STEP * jnp.concatenate(wets, axis=0) * heating
        if step < STEPS - 1:
            target, base = state.at[step + 1], Y + c * piece
        else:
            target, base = final, c * piece
        for x in range(deep):
            target[pl.ds(0, tracers), pl.ds(base + x * Y, Y), :] = result[
                :, x * wide : (x + 1) * wide
            ].reshape(tracers, Y, wide)
        target[tracers, pl.ds(base, piece), :] = heat

    for step in range(STEPS):
        for c in order:
            for side in (NORTH, SOUTH):
                halos[step, c, side].wait_recv()
            if c == 0:
                halos[step, chunks - 1, EAST].wait_recv()
            if c == chunks - 1:
                halos[step, 0, WEST].wait_recv()
            advance(step, c)
            if step < STEPS - 1:
                exchange(step + 1, c)
            else:
                leave(c)
    for copy in leaving:
        copy.wait()
    for copy in sent + list(arriving.values()):
        copy.wait_send()

SHARE = 5
FIRST = 3


def wide_halves(x):
    high, low = halves(x)
    return jnp.concatenate([high, high, low], axis=1)


def tall_halves(x):
    high, low = halves(x)
    return jnp.concatenate([high, low, high], axis=0)


def pair_tables(rates_ref, yields_ref, tracers, wide, Y):
    rows = tracers * Y
    spread = (iota((rows, tracers), 0) // Y == iota((rows, tracers), 1)).astype(jnp.float32)
    same = iota((rows, rows), 0) % Y == iota((rows, rows), 1) % Y
    full = exact_dot(exact_dot(spread, rates_ref[...]), spread, ((1,), (1,)))
    full = jnp.where(same, full, 0.0) * REACT_STEP
    diagonal = (iota((rows, rows), 0) == iota((rows, rows), 1)).astype(jnp.float32)
    one = diagonal + full
    two = exact_dot(one, one)
    three = exact_dot(two, one)
    four = exact_dot(two, two)
    source = [
        exact_dot(spread * yields_ref[...], jnp.ones((tracers, wide), jnp.float32)) * REACT_STEP
    ]
    for power in (one, two, three):
        source.append(exact_dot(power, source[0]))
    powers = jnp.concatenate([power[: 3 * Y] for power in (one, two, three)] + [four], axis=0)
    shape = (rows, wide)
    lane = iota(shape, 1)
    inject = jnp.zeros(shape, jnp.float32)
    for sub in range(SUB):
        hit = jnp.logical_and(lane // Y == sub, lane % Y == iota(shape, 0) % Y)
        inject = inject + jnp.where(hit, source[SUB - 1 - sub], 0.0)
    return (
        wide_halves(powers),
        wide_halves(inject[:, : SUB * Y]),
        [v[: 3 * Y] for v in source],
    )


def pair_plan(half):
    low = -SHARE - STEPS
    ranges = [(half - STEPS, STEPS)]
    for at, end in ((SHARE - STEPS, half - STEPS), (low, SHARE - STEPS)):
        while at < end:
            size = min(STEPS, end - at)
            ranges.append((at, size))
            at += size
    return low, ranges


def pair_kernel(
    regions, sects,
    solute, heat_hbm, east_hbm, north_hbm, layers_hbm, rates_hbm, yields_hbm,
    tracers_out, heat_out,
    layers_in, rates_ref, yields_ref, state, coef, wets, final, measure,
    send_sem, recv_sem, go_sem,
):
    groups = 2
    region, group, sect = (lax.axis_index(a) for a in ("region", "tracer", "sect"))
    own, X, Y, wide = solute.shape
    half = X // groups
    tracers = own * groups
    fields = tracers + 1
    base = STEPS + 1
    low, ranges = pair_plan(half)
    reach = half - low
    odd = region % 2
    part = group + odd * (1 - 2 * group)
    peer = 1 - group

    def pick(flag, a, b):
        return a + flag * (b - a)

    def P(u, k, flag=part):
        return pick(flag, half + STEPS - u - k, u - low)

    def B(u, k, flag=part):
        return pick(flag, half - u - k, half + u)

    outer_region = lax.rem(region + pick(part, regions - 1, 1), regions)
    outer_part = 1 - part
    outer_odd = outer_region % 2
    beside = {"region": outer_region, "tracer": outer_part + outer_odd * (1 - 2 * outer_part)}
    north = {"sect": lax.rem(sect + 1, sects)}
    south = {"sect": lax.rem(sect + sects - 1, sects)}
    across = {"tracer": peer}
    mine, other = pl.ds(group * own, own), pl.ds(peer * own, own)

    names, lines = {}, {}

    def slot(name):
        return names.setdefault(name, len(names))

    def tally(name, ref):
        lines[name] = lines.get(name, 0) + math.prod(ref.shape) // wide

    def settle(name, sems=recv_sem):
        some = measure.at[pl.ds(0, lines[name])]
        at = slot(name) if sems is recv_sem else int(name[4:])
        with jax.named_scope(name):
            pltpu.make_async_copy(some, some, sems.at[at]).wait()

    def local(name, source_ref, target_ref):
        tally(name, target_ref)
        pltpu.make_async_copy(source_ref, target_ref, recv_sem.at[slot(name)]).start()

    def remote(name, source_ref, target_ref, device, turn=0):
        tally(name, target_ref)
        tally(f"sent{turn}", source_ref)
        push(name, source_ref, target_ref, device, turn)

    def push(name, source_ref, target_ref, device, turn=0):
        pltpu.make_async_remote_copy(
            src_ref=source_ref,
            dst_ref=target_ref,
            send_sem=send_sem.at[turn],
            recv_sem=recv_sem.at[slot(name)],
            device_id=device,
            device_id_type=MESH,
        ).start()

    raw = state.at[0]
    body = pl.ds(base, Y)
    blank = jnp.zeros((tracers + 4, 1, STEPS, wide), jnp.float32)
    for u in (low, half, half + 1, half + 2):
        for row in (base - STEPS, base + Y):
            raw[:, pl.ds(P(u, 1), 1), pl.ds(row, STEPS), :] = blank
    barrier = pltpu.get_barrier_semaphore()
    @pl.when(part == 0)
    def _():
        pl.semaphore_signal(barrier, inc=1, device_id=beside, device_id_type=MESH)

    for device in (across, north, south):
        pl.semaphore_signal(barrier, inc=1, device_id=device, device_id_type=MESH)

    small = [
        pltpu.make_async_copy(source_ref, target_ref, recv_sem.at[slot(f"small{i}")])
        for i, (source_ref, target_ref) in enumerate(
            ((layers_hbm, layers_in), (rates_hbm, rates_ref), (yields_hbm, yields_ref))
        )
    ]
    for copy in small:
        copy.start()
    p_all, b_all = P(low, reach), B(low, reach)
    in_block = pl.ds(b_all, reach)
    in_state = pl.ds(p_all, reach)
    extra = ((heat_hbm, tracers), (east_hbm, fields), (north_hbm, fields + 1))
    local("loads", solute.at[:, in_block], raw.at[mine, in_state, body])
    for ref, field in extra:
        local("loads", ref.at[in_block], raw.at[field, in_state, body])

    with jax.named_scope("barrier"):
        pl.semaphore_wait(barrier, 3 + part)

    def cross(i):
        u, k = ranges[i]
        remote(
            f"x{i}",
            solute.at[:, pl.ds(B(u, k, 1 - part), k)],
            raw.at[mine, pl.ds(P(u, k, 1 - part), k), body],
            across,
        )

    edge = half - STEPS
    edge_block = pl.ds(B(edge, STEPS), STEPS)
    edge_state = pl.ds(P(edge, STEPS), STEPS)
    past = pl.ds(pick(part, reach, 0), STEPS)
    cross(0)
    edges = [(solute.at[:, edge_block], raw.at[mine, past, body])]
    edges += [(ref.at[edge_block], raw.at[field, past, body]) for ref, field in extra]
    for source_ref, target_ref in edges:
        tally("outer", target_ref)
        tally("sent0", source_ref)

    @pl.when(part == 1)
    def _():
        pl.semaphore_signal(go_sem, inc=1, device_id=beside, device_id_type=MESH)
        for source_ref, target_ref in edges:
            push("outer", source_ref, target_ref, beside)

    for i in range(1, len(ranges)):
        cross(i)
    far = sect % 2

    def both_sides(send):
        for first in (0, 1):
            @pl.when(far == first)
            def _():
                for side in (first, 1 - first):
                    send(side, (south, north)[side])

    def halo_row(side, deep=STEPS):
        return pl.ds(base - deep if side else base + Y, deep)

    def tally_sides(name, refs):
        for ref in refs:
            for _ in range(2):
                tally(name, ref)
                tally("sent0", ref)

    def direct_rows(name, u, k):
        b, p = pl.ds(B(u, k), k), pl.ds(P(u, k), k)
        refs = [(solute.at[:, b], mine)] + [(ref.at[b], field) for ref, field in extra]

        def send(side, device):
            block_rows = pl.ds(Y - STEPS if side else 0, STEPS)
            for ref, field in refs:
                rows = ref.at[:, :, block_rows] if ref is refs[0][0] else ref.at[:, block_rows]
                push(name, rows, raw.at[field, p, halo_row(side)], device)

        both_sides(send)
        tally_sides(name, [raw.at[field, p, halo_row(0)] for _, field in refs])

    def beside_rows(name, some, u, k, deep=STEPS):
        place = pl.ds(P(u, k), k)

        def send(side, device):
            start = base + Y - deep if side else base
            push(
                name,
                raw.at[some, place, pl.ds(start, deep)],
                raw.at[some, place, halo_row(side, deep)],
                device,
            )

        both_sides(send)
        tally_sides(name, [raw.at[some, place, halo_row(0, deep)]])

    near = 1 + -(-(FIRST + 2 * STEPS) // STEPS)
    cone = min((near - 1) * STEPS, edge + STEPS + STEPS - SHARE)
    cone_at = max(low + 1, SHARE - STEPS)
    cone_end = SHARE - STEPS + cone
    direct_rows("rows", cone_at, cone_end - cone_at)
    if cone_end < half:
        direct_rows("rest", cone_end, half - cone_end)

    for copy in small:
        copy.wait()
    total = X * Y
    pick_rows = iota((total, X), 0) // Y == iota((total, X), 1)
    depth = lax.dot_general(
        pick_rows.astype(jnp.bfloat16),
        layers_in[...].astype(jnp.float32).astype(jnp.bfloat16),
        (((1,), (1,)), ((), ())),
        preferred_element_type=jnp.float32,
    )
    depth = jnp.where(iota((total, Y), 0) % Y == iota((total, Y), 1), depth, 0.0)
    depth = half_dot(depth.astype(jnp.bfloat16), jnp.ones((Y, wide), jnp.bfloat16))
    wets[...] = (iota((total, wide), 1).astype(jnp.float32) < depth).astype(jnp.float32).reshape(
        X, Y, wide
    )
    wet_field = fields + 2
    raw[wet_field, in_state, body, :] = wets[in_block]
    beside_rows("rows", pl.ds(wet_field, 1), low + 1, reach - 1)

    with jax.named_scope("make_tables"):
        powers, inject, source = pair_tables(rates_ref, yields_ref, tracers, wide, Y)
    @pl.when(part == 0)
    def _():
        pl.semaphore_wait(go_sem, 1)
        for source_ref, target_ref in edges:
            push("outer", source_ref, target_ref, beside)

    remote("outer", raw.at[wet_field, edge_state, body], raw.at[wet_field, past, body], beside)
    shape = (wide, wide)
    upper = (iota(shape, 0) < iota(shape, 1)).astype(jnp.float32)
    upper = upper + 0.5 * (iota(shape, 0) == iota(shape, 1)).astype(jnp.float32)
    upper = jnp.concatenate([upper.astype(jnp.bfloat16)] * 2, axis=0)
    level = (iota((Y, wide), 1).astype(jnp.float32) + 0.5) * (-WATER_ATT / wide)
    settle("loads")

    def light(chl_abs):
        high, low_part = halves(chl_abs)
        above = half_dot(jnp.concatenate([high, low_part], axis=1), upper)
        tall = jnp.concatenate([level] * (chl_abs.shape[0] // Y), axis=0)
        return jnp.exp(tall - CHL_ATT / wide * above)

    done = set()

    def once(name):
        fresh = name not in done
        done.add(name)
        return fresh

    def arrive(i):
        if once(f"x{i}"):
            settle(f"x{i}")
            u, k = ranges[i]
            some = pl.ds(P(u, k), k)
            if i == 0:
                remote("outer", raw.at[other, some, body], raw.at[other, past, body], beside)
            skip = int(u == low)
            beside_rows(f"y{i}", other, u + skip, k - skip)
            if i == near - 1 and low + 1 < cone_at:
                direct_rows("inner", low + 1, cone_at - low - 1)

    def arrive_outer():
        arrive(0)
        if once("outer"):
            settle("outer")
            beside_rows("corner", slice(None), half, STEPS - 1, STEPS - 1)

    def ready(first, last):
        if once("rows"):
            settle("rows")
        for name, wanted in (("inner", first < cone_at), ("rest", last >= cone_end)):
            if wanted and name in lines and once(name):
                settle(name)
        for i, (u, k) in enumerate(ranges):
            if u <= last and first < u + k:
                arrive(i)
                if once(f"y{i}"):
                    settle(f"y{i}")
        if last >= half:
            arrive_outer()
            if once("corner"):
                settle("corner")

    windows = [
        (base - STEPS + 1, base + Y + STEPS - 1 - Y),
        (base - 1, base + 1),
        (base,),
    ]

    def stencil(step, p, r):
        here = pl.ds(r, Y)
        up_rows, down_rows = pl.ds(r + 1, Y), pl.ds(r - 1, Y)
        if step == 0:
            wet = raw[wet_field, p, here, :]
            south_wet = raw[wet_field, p, down_rows, :]
            east = raw[fields, p, here, :] * wet * raw[wet_field, p + 1, here, :]
            west = raw[fields, p - 1, here, :] * raw[wet_field, p - 1, here, :] * wet
            up = raw[fields + 1, p, here, :] * wet * raw[wet_field, p, up_rows, :]
            down = raw[fields + 1, p, down_rows, :] * south_wet * wet
            scaled = TIME_STEP * wet
            c = [
                wet
                - scaled
                * (
                    jnp.maximum(east, 0.0) - jnp.minimum(west, 0.0)
                    + jnp.maximum(up, 0.0) - jnp.minimum(down, 0.0)
                ),
                -scaled * jnp.minimum(east, 0.0),
                scaled * jnp.maximum(west, 0.0),
                -scaled * jnp.minimum(up, 0.0),
                scaled * jnp.maximum(down, 0.0),
                scaled,
            ]
            for i, v in enumerate(c):
                coef[i, p, here, :] = v
        else:
            c = [coef[i, p, here, :] for i in range(6)]
        some = pl.ds(0, fields)
        moved = (
            c[0] * state[step, some, p, here, :]
            + c[1] * state[step, some, p + 1, here, :]
            + c[2] * state[step, some, p - 1, here, :]
            + c[3] * state[step, some, p, up_rows, :]
            + c[4] * state[step, some, p, down_rows, :]
        )
        return moved, c[5]

    def advance(*work):
        work = [item for item in work if item[2] > 0]
        for step, u, k in work:
            if step == 0:
                ready(u - 1, u + k)
        with jax.named_scope("go" + "_".join(f"{s}:{u}:{k}" for s, u, k in work)):
            compute(work)

    def compute(work):
        tiles = []
        for step, u, k in work:
            p = P(u, k)
            for i in range(k):
                for r in windows[step]:
                    tiles.append((step, p + i, r))
        columns, heats, scales = [], [], []
        for step, p, r in tiles:
            moved, scaled = stencil(step, p, r)
            columns.append(moved[:tracers].reshape(tracers * Y, wide))
            heats.append(moved[tracers])
            scales.append(scaled)
        n = len(tiles)
        mixed = jnp.concatenate(columns, axis=1)
        parts = tall_halves(mixed)
        block = 3 * Y
        if n <= 2 * STEPS:
            ahead = half_dot(powers[: 3 * block], parts)
            result = half_dot(powers[3 * block :], parts)
        else:
            ahead = half_dot(powers, parts)
            result = ahead[3 * block :]

        def part_of(rows, i):
            return stack(rows[i * Y : (i + 1) * Y], wide)

        def spread(v, i):
            return jnp.concatenate([v[i * Y : (i + 1) * Y]] * n, axis=0)

        rates = []
        for sub in range(SUB):
            rows = mixed[:block] if sub == 0 else ahead[(sub - 1) * block : sub * block]
            value = []
            for i in range(3):
                v = part_of(rows, i)
                for j, rate in enumerate(rates):
                    v = v + spread(source[sub - 1 - j], i) * rate
                value.append(v)
            nutrient, chl, phyto = value
            rates.append(
                light(jnp.abs(chl)) * (nutrient / (jnp.abs(nutrient) + HALF_SAT) * phyto)
            )
        chl = part_of(result, 1)
        for j, rate in enumerate(rates):
            chl = chl + spread(source[SUB - 1 - j], 1) * rate
        chl_abs = jnp.abs(chl)
        flat = jnp.concatenate([unstack(rate, Y) for rate in rates], axis=0)
        result = result + half_dot(inject, tall_halves(flat))
        heat = jnp.concatenate(heats, axis=0) + HEAT_GAIN * (
            jnp.concatenate(scales, axis=0) * chl_abs * light(chl_abs)
        )
        for i, (step, p, r) in enumerate(tiles):
            value = result[:, i * wide : (i + 1) * wide].reshape(tracers, Y, wide)
            if step < STEPS - 1:
                here = pl.ds(r, Y)
                state[step + 1, pl.ds(0, tracers), p, here, :] = value
                state[step + 1, tracers, p, here, :] = heat[i * Y : (i + 1) * Y]
            else:
                final[pl.ds(0, tracers), p, :, :] = value
                final[tracers, p, :, :] = heat[i * Y : (i + 1) * Y]

    def leave(u, k):
        if k <= 0:
            return
        some, place = pl.ds(P(u, k), k), pl.ds(B(u, k), k)
        if u >= SHARE:
            remote("arrivals", final.at[other, some], tracers_out.at[:, place], across, 1)
            remote("arrivals", final.at[tracers, some], heat_out.at[place], across, 1)
        local("leaving", final.at[mine, some], tracers_out.at[:, place])
        local("leaving", final.at[tracers, some], heat_out.at[place])

    for action in schedule(half):
        if action[0] == "x":
            arrive(action[1])
        elif action[0] == "z":
            arrive_outer()
        elif action[0] == "go":
            advance(*action[1:])
        else:
            leave(*action[1:])
    settle("leaving")
    settle("arrivals")
    settle("sent0", send_sem)
    settle("sent1", send_sem)


def schedule(half):
    count = len(pair_plan(half)[1])
    h, a, b = SHARE, FIRST, half - STEPS
    near = 1 + -(-(a + 2 * STEPS) // STEPS)
    inner = [[(s, -h - 2 + s, 2 * h)] if h else [] for s in range(STEPS)]
    own = 1 + -(-(b - h + STEPS) // STEPS)
    rest = b - h - a
    late = [("x", i) for i in range(own, count)]
    plan = [("x", i) for i in range(own)]
    plan += [("go", (0, h - 2, a + 4)), ("z",), *late[:1], ("go", (1, h - 1, a + 2)), *late[1:2]]
    plan += [("go", (2, h, a), (0, h + a + 2, rest)), ("out", h, a)]
    plan += [*late[2:], ("go", (1, h + a + 1, rest), (0, b + 2, 3))]
    plan += [("go", (2, h + a, rest), (1, b + 1, 3)), ("out", h + a, rest)]
    plan += [("go", (2, b, 3)), ("out", b, 3)]
    for s in range(STEPS if h else 0):
        plan.append(("go", *inner[s]))
    return plan + ([("out", -h, 2 * h)] if h else [])


def paired(shape, groups, regions, sects):
    return (
        groups == 2 and regions > 1 and regions % 2 == 0 and sects > 1
        and shape[2] == 8 and shape[3] == 128 and shape[1] % 2 == 0 and shape[1] >= 24
        and shape[0] * groups * shape[2] == 128
    )


def write_out(mixture, heat, mixture_out, heat_out, sems):
    copies = [pltpu.make_async_copy(mixture, mixture_out, sems.at[0])]
    copies.append(pltpu.make_async_copy(heat, heat_out, sems.at[1]))
    for copy in copies:
        copy.start()
    for copy in copies:
        copy.wait()


def pair_call(solute, thermal, eastward, northward, layers, rates, yields, regions, sects):
    own, X, Y, wide = solute.shape
    tracers = own * 2
    half = X // 2
    low, ranges = pair_plan(half)
    columns = half - low + STEPS
    operands = [
        pltpu.with_memory_space_constraint(v, pltpu.HBM)
        for v in (solute, thermal, eastward, northward, layers.T, rates, yields.reshape(1, tracers))
    ]
    hbm = pl.BlockSpec(memory_space=pltpu.HBM)
    free = pl.BlockSpec(memory_space=pl.ANY)
    dma = pltpu.SemaphoreType.DMA
    mixture, heat = pl.pallas_call(
        functools.partial(pair_kernel, regions, sects),
        out_shape=(
            jax.ShapeDtypeStruct(solute.shape, jnp.float32),
            jax.ShapeDtypeStruct(thermal.shape, jnp.float32),
        ),
        in_specs=[hbm] * 7,
        out_specs=(free, free),
        scratch_shapes=[
            pltpu.VMEM((Y, X), jnp.int32),
            pltpu.VMEM((tracers, tracers), jnp.float32),
            pltpu.VMEM((1, tracers), jnp.float32),
            pltpu.VMEM((STEPS, tracers + 4, columns, 2 * Y, wide), jnp.float32),
            pltpu.VMEM((6, columns, 2 * Y, wide), jnp.float32),
            pltpu.VMEM((X, Y, wide), jnp.float32),
            pltpu.VMEM((tracers + 1, columns, Y, wide), jnp.float32),
            pltpu.VMEM((MEASURE, wide), jnp.float32),
            dma((2,)),
            dma((len(ranges) * 2 + 11,)),
            pltpu.SemaphoreType.REGULAR,
        ],
        compiler_params=pltpu.CompilerParams(
            collective_id=0, has_side_effects=True, vmem_limit_bytes=40 << 20
        ),
    )(*operands)
    return pl.pallas_call(
        write_out,
        out_shape=(
            jax.ShapeDtypeStruct(solute.shape, jnp.float32),
            jax.ShapeDtypeStruct(thermal.shape, jnp.float32),
        ),
        in_specs=[free] * 2,
        out_specs=(hbm, hbm),
        scratch_shapes=[dma((2,))],
        compiler_params=pltpu.CompilerParams(vmem_limit_bytes=1 << 20),
    )(mixture, heat)


MEASURE = 8192


def solution(mesh):
    regions, groups, sects = (mesh.shape[a] for a in ("region", "tracer", "sect"))

    def body(solute, thermal, eastward, northward, layers, rates, yields):
        if paired(solute.shape, groups, regions, sects):
            return pair_call(
                solute, thermal, eastward, northward, layers, rates, yields, regions, sects
            )
        own, rows, cols, wide = solute.shape
        tracers = own * groups
        span = rows // groups
        fields = tracers + 1
        flat = (rows * cols, wide)
        free, hbm = pl.BlockSpec(memory_space=pl.ANY), pl.BlockSpec(memory_space=pltpu.HBM)
        dma = pltpu.SemaphoreType.DMA
        peers = max(groups - 1, 1)
        chunks = plan(span)[0]
        mixture, heat = pl.pallas_call(
            functools.partial(kernel, regions, groups, sects),
            out_shape=(
                jax.ShapeDtypeStruct((own, *flat), jnp.float32),
                jax.ShapeDtypeStruct(flat, jnp.float32),
            ),
            in_specs=[hbm] * 7,
            out_specs=(free, free),
            scratch_shapes=[
                pltpu.VMEM((cols, rows), jnp.int32),
                pltpu.VMEM((tracers, tracers), jnp.float32),
                pltpu.VMEM((1, tracers), jnp.float32),
                pltpu.VMEM((STEPS, fields + 3, (span + 2) * cols, wide), jnp.float32),
                pltpu.VMEM((STEPS, chunks, 2, fields + 3, span // chunks, wide), jnp.float32),
                pltpu.VMEM((STEPS, chunks, 2, fields + 3, span // chunks, wide), jnp.float32),
                pltpu.VMEM((6, *flat), jnp.float32),
                pltpu.VMEM((fields, span * cols, wide), jnp.float32),
                dma((peers, chunks)),
                dma((peers, chunks)),
                dma((STEPS, chunks, 4)),
                dma((STEPS, chunks, 4)),
                dma((peers, chunks, 2)),
                dma((peers, chunks, 2)),
                dma((chunks, 3)),
                dma((6,)),
            ],
            compiler_params=pltpu.CompilerParams(
                collective_id=0, has_side_effects=True, vmem_limit_bytes=60 << 20
            ),
        )(
            solute.reshape(own, *flat),
            thermal.reshape(flat),
            eastward.reshape(flat),
            northward.reshape(flat),
            layers.T,
            rates,
            yields.reshape(1, tracers),
        )
        return mixture.reshape(solute.shape), heat.reshape(thermal.shape)

    return jax.shard_map(
        body,
        mesh=mesh,
        in_specs=(
            P("tracer", "region", "sect", None),
            P("region", "sect", None),
            P("region", "sect", None),
            P("region", "sect", None),
            P("region", "sect"),
            P(),
            P(),
        ),
        out_specs=(P("tracer", "region", "sect", None), P("region", "sect", None)),
        check_vma=False,
    )
```
